128 devices in a mesh: gx: 16 (over z, y), gy: 8 (over x, core).
Axes of the slice: x: 4, y: 4, z: 4, core: 2. Of those that a mesh axis runs over, the one named last changes fastest.
Arguments:
- rhs_field: float32 [3, 32, 64, 4096], P(None, None, 'gy', 'gx'), may hold values from -6 to 6
- couplings: float32 [6, 3, 3, 32, 64, 4096], P(None, None, None, None, 'gy', 'gx'), may hold values from -0.6 to 0.6
- pivot_inverses: float32 [3, 3, 32, 64, 4096], P(None, None, None, 'gy', 'gx'), may hold values from -3.5 to 3.5
- colours: int32 [32, 64, 4096], P(None, 'gy', 'gx'), may hold values from 0 to 3
- perf_cells: int32 [131072], P(('gx', 'gy')), may hold values from 0 to 65535
- perf_wells: int32 [131072], P(('gx', 'gy')), may hold values from 0 to 8191, as said below
- perf_segments: int32 [131072], P(('gx', 'gy')), may hold values from 0 to 15
- perf_gather: float32 [3, 131072], P(None, ('gx', 'gy')), may hold values from -3 to 3
- perf_return: float32 [3, 131072], P(None, ('gx', 'gy')), may hold values from -3 to 3
- well_slot: int32 [8192], replicated, may hold values from 0 to 8191, as said below
- seg_count: int32 [8192], replicated, may hold values from 1 to 16
- well_inverses: float32 [8192, 16, 16], P(('gx', 'gy')), may hold values from -1.5 to 1.5
Outputs:
- precond_field: float32 [3, 32, 64, 4096], P(None, None, 'gy', 'gx')
The draws below stay inside these ranges and needn't reach their ends.
Inputs may be any that keep to these rules, and one draw needn't show every extreme that they name: `well_slot`: wells are numbered by owner: well w's slot lies in w // 64 * 64 to that plus 64 - 1, each slot taken once, so slot s belongs to tile s // 64 (tiles ordered with x slowest). `perf_wells`: A perforation listed with a tile may name a well of any owner.
All inputs are finite; a program needn't handle non-finite values.
Results may differ from the reference program's by a relative error of at most 0.0001.
Values sent between devices are 32-bit elements; how exact they have to be, the bound alone decides.
No kernel may reach another device: no remote copies, remote signals or barrier semaphores. Data moves between devices by JAX's collectives and lax.ppermute only.
A program may use at most 384 MiB of HBM per device.

```python
import jax
import jax.numpy as jnp
from jax import lax

CX = 256
CY = 8
NZ = 32
SEG = 16
WELL_DEV = 64
PERF_DEV = 1024
NX = 4096
NY = 64
CELLS_DEV = 65536
PERFS = 131072
WELLS = 8192
N_GY = 8
DEVICES = 128


def draw_perf_wells(key, part):
    index = jnp.arange(PERFS, dtype=jnp.int32)
    tile = index // PERF_DEV
    within = index % PERF_DEV
    owner_far = (tile + DEVICES // 2) % DEVICES
    owner_before = (tile + DEVICES - 1) % DEVICES
    owner_any = jax.random.randint(jax.random.fold_in(key, 11), (PERFS,), 0, DEVICES, dtype=jnp.int32)
    owner = jnp.where(within == 0, owner_far, jnp.where(within == 1, owner_before, owner_any))
    first = jax.random.randint(jax.random.fold_in(key, 12), (PERFS,), 0, WELL_DEV, dtype=jnp.int32)
    second = jax.random.randint(jax.random.fold_in(key, 13), (PERFS,), 0, WELL_DEV, dtype=jnp.int32)
    local_well = jnp.minimum(first, second)
    return (owner * WELL_DEV + local_well).astype(jnp.int32)


def draw_well_slot(key, part):
    blocks = jnp.arange(DEVICES, dtype=jnp.int32)

    def one_block(block):
        order = jax.random.permutation(jax.random.fold_in(jax.random.fold_in(key, 21), block), WELL_DEV)
        return (block * WELL_DEV + order).astype(jnp.int32)
    return jax.vmap(one_block)(blocks).reshape(-1).astype(jnp.int32)


def touch_ends(drawn, stream_key, smallest, high):
    longest = drawn.shape.index(max(drawn.shape))
    spots = []
    for shift in (0, 1):
        where = [jax.random.randint(jax.random.fold_in(stream_key, axis), (), 0, length) for axis, length in enumerate(drawn.shape)]
        where[longest] = (where[longest] + shift) % drawn.shape[longest]
        spots.append(tuple(where))
    return drawn.at[spots[0]].set(smallest).at[spots[1]].set(high)


def steps_of(stream_key, extent, split, least, top_value):
    def one(position, parts):
        heights = jax.random.uniform(jax.random.fold_in(jax.random.fold_in(stream_key, 6), position), (parts,), jnp.float32, least / len(split), top_value / len(split))
        return jnp.repeat(jnp.exp(heights), extent[position] // parts).reshape((-1,) + (1,) * (len(extent) - position - 1))

    gain = one(*split[0])
    for cut in split[1:]:
        gain = gain * one(*cut)
    return gain


def gaussian(stream_key, extent, deviation, most, split=(), kind=jnp.bfloat16):
    gain = steps_of(stream_key, extent, split, -0.22, 0.18) if split else 1.0
    result = jax.random.normal(stream_key, extent, jnp.float32) * deviation * gain
    return jnp.minimum(jnp.maximum(result, -most), most).astype(kind)


def setup_inputs(seed: int = 0) -> dict:
    arg_keys = jax.random.split(jax.random.key(seed), 13)
    rhs_field = gaussian(arg_keys[0], (3, NZ, NY, NX), 1.0, 6.0, ((2, 8), (3, 16)), jnp.float32)
    couplings = gaussian(arg_keys[1], (6, 3, 3, NZ, NY, NX), 0.12, 0.6, ((4, 8), (5, 16)), jnp.float32)
    pivot_inverses = gaussian(arg_keys[2], (3, 3, NZ, NY, NX), 3 ** -0.5, 3.5, ((3, 8), (4, 16)), jnp.float32)
    colours = touch_ends(jax.random.randint(arg_keys[3], (NZ, NY, NX), 0, 4), jax.random.fold_in(arg_keys[3], 1), 0, 3).astype(jnp.int32)
    perf_cells = touch_ends(jax.random.randint(arg_keys[4], (PERFS,), 0, CELLS_DEV), jax.random.fold_in(arg_keys[4], 1), 0, CELLS_DEV - 1).astype(jnp.int32)
    perf_wells = draw_perf_wells(jax.random.fold_in(arg_keys[12], 71), 0)
    perf_segments = touch_ends(jax.random.randint(arg_keys[6], (PERFS,), 0, SEG), jax.random.fold_in(arg_keys[6], 1), 0, SEG - 1).astype(jnp.int32)
    perf_gather = gaussian(arg_keys[7], (3, PERFS), 0.5, 3.0, ((1, 128),), jnp.float32)
    perf_return = gaussian(arg_keys[8], (3, PERFS), 0.5, 3.0, ((1, 128),), jnp.float32)
    well_slot = draw_well_slot(jax.random.fold_in(arg_keys[12], 71), 0)
    seg_count = touch_ends(jax.random.randint(arg_keys[10], (WELLS,), 1, SEG + 1), jax.random.fold_in(arg_keys[10], 1), 1, SEG).astype(jnp.int32)
    well_inverses = gaussian(arg_keys[11], (WELLS, SEG, SEG), SEG ** -0.5, 1.5, ((0, 128),), jnp.float32)
    return {"rhs_field": rhs_field, "couplings": couplings, "pivot_inverses": pivot_inverses, "colours": colours, "perf_cells": perf_cells, "perf_wells": perf_wells, "perf_segments": perf_segments, "perf_gather": perf_gather, "perf_return": perf_return, "well_slot": well_slot, "seg_count": seg_count, "well_inverses": well_inverses}


def couple(couplings, field):
    padded = jnp.pad(field, ((0, 0), (1, 1), (1, 1), (1, 1)))
    beside = jnp.stack([padded[:, 1:-1, 1:-1, :-2], padded[:, 1:-1, 1:-1, 2:], padded[:, 1:-1, :-2, 1:-1], padded[:, 1:-1, 2:, 1:-1], padded[:, :-2, 1:-1, 1:-1], padded[:, 2:, 1:-1, 1:-1]])
    return jnp.sum(couplings * beside[:, None], axis=(0, 2))


def pivot(pivot_inverses, field):
    return jnp.sum(pivot_inverses * field[None], axis=1)


def well_solve(inverses, totals, seg_counts):
    seg_index = jnp.arange(totals.shape[1], dtype=jnp.int32)
    alive_mask = (seg_index[None, :] < seg_counts[:, None]).astype(jnp.float32)
    return alive_mask * jnp.einsum("wst,wt->ws", inverses, alive_mask * totals, precision=lax.Precision.HIGHEST)


def reference(rhs_field, couplings, pivot_inverses, colours, perf_cells, perf_wells, perf_segments, perf_gather, perf_return, well_slot, seg_count, well_inverses):
    lower = jnp.zeros_like(rhs_field)
    upper_in = jnp.zeros_like(rhs_field)
    for colour in range(4):
        chosen = (colours == colour)[None]
        if colour == 0:
            current = rhs_field
        else:
            current = rhs_field - couple(couplings, lower)
        upper_in = jnp.where(chosen, current, upper_in)
        lower = jnp.where(chosen, pivot(pivot_inverses, current), lower)
    sweep_field = jnp.zeros_like(rhs_field)
    for colour in (3, 2, 1, 0):
        chosen = (colours == colour)[None]
        if colour == 3:
            current = pivot(pivot_inverses, upper_in)
        else:
            current = pivot(pivot_inverses, upper_in - couple(couplings, sweep_field))
        sweep_field = jnp.where(chosen, current, sweep_field)
    device = (jnp.arange(PERFS, dtype=jnp.int32) // PERF_DEV).astype(jnp.int32)
    tile_x = device // N_GY
    tile_y = device % N_GY
    layer = perf_cells // (CY * CX)
    row_y = tile_y * CY + (perf_cells // CX) % CY
    row_x = tile_x * CX + perf_cells % CX
    at_cells = sweep_field[:, layer, row_y, row_x]
    terms = jnp.sum(perf_gather * at_cells, axis=0)
    well_key = (well_slot[perf_wells] * SEG + perf_segments).astype(jnp.int32)
    totals = jnp.zeros((WELLS * SEG,), jnp.float32).at[well_key].add(terms).reshape(WELLS, SEG)
    slot_counts = jnp.zeros((WELLS,), jnp.int32).at[well_slot].set(seg_count)
    segment_values = well_solve(well_inverses, totals, slot_counts)
    at_perfs = segment_values.reshape(-1)[well_key]
    return sweep_field.at[:, layer, row_y, row_x].add(-perf_return * at_perfs[None])
```

```python
import jax
import jax.numpy as jnp
from jax import lax
from jax.experimental import pallas as pl
from jax.experimental.pallas import tpu as pltpu
from jax.sharding import PartitionSpec as P

F32 = jnp.float32
BF16 = jnp.bfloat16
VMEM_SPEC = pl.BlockSpec(memory_space=pltpu.VMEM)
SMEM_SPEC = pl.BlockSpec(memory_space=pltpu.SMEM)


def iota(shape, dim):
    return lax.broadcasted_iota(jnp.int32, shape, dim)


def split3(x):
    a = x.astype(BF16)
    r = x - a.astype(F32)
    b = r.astype(BF16)
    c = (r - b.astype(F32)).astype(BF16)
    return a, b, c


def dot(a, b, dims):
    return lax.dot_general(a, b, (dims, ((), ())), preferred_element_type=F32)


def in_vmem(x):
    return pltpu.with_memory_space_constraint(x, pltpu.VMEM)


def call(body, outs, ins, smem=0, name=None, cost=None, limit=None):
    specs = [SMEM_SPEC] * smem + [VMEM_SPEC] * (len(ins) - smem)
    args = list(ins[:smem]) + [in_vmem(x) for x in ins[smem:]]
    return pl.pallas_call(
        body,
        out_shape=tuple(pltpu.VMEM(s, d) for s, d in outs),
        in_specs=specs,
        out_specs=tuple(VMEM_SPEC for _ in outs),
        compiler_params=pltpu.CompilerParams(vmem_limit_bytes=limit or (8 << 20)),
        cost_estimate=cost,
        name=name,
    )(*args)


def emit_edges(new, z, nz, edges, ylo_ref, yhi_ref):
    xlo, xhi = edges
    lane = iota((8, 128), 1)
    for j in range(3):
        at = j * nz + z
        xlo = jnp.where(lane == at, pltpu.roll(new[j][:, :128], at, 1), xlo)
        xhi = jnp.where(lane == at, pltpu.roll(new[j][:, -128:], (at + 1) % 128, 1), xhi)
        ylo_ref[pl.ds(at, 1), :] = new[j][0:1, :]
        yhi_ref[pl.ds(at, 1), :] = new[j][-1:, :]
    return xlo, xhi


def zero_ends(ref, nz):
    zero = jnp.zeros(ref.shape[2:], F32)
    for j in range(3):
        ref[j, 0] = zero
        ref[j, nz + 1] = zero


def first_body(rhs_ref, piv_ref, col_ref, v_ref, xlo_ref, xhi_ref, ylo_ref, yhi_ref):
    nz = rhs_ref.shape[1]
    zero_ends(v_ref, nz)

    def step(z, edges):
        rhs = [rhs_ref[j, z] for j in range(3)]
        chosen = col_ref[z] == 0
        new = []
        for i in range(3):
            p = piv_ref[i, 0, z] * rhs[0] + piv_ref[i, 1, z] * rhs[1] + piv_ref[i, 2, z] * rhs[2]
            p = jnp.where(chosen, p, 0.0)
            v_ref[i, z + 1] = p
            new.append(p)
        return emit_edges(new, z, nz, edges, ylo_ref, yhi_ref)

    zero = jnp.zeros((8, 128), F32)
    xlo, xhi = lax.fori_loop(0, nz, step, (zero, zero))
    xlo_ref[...] = xlo
    xhi_ref[...] = xhi


def turn_body(colour, forward, final, *refs):
    (meta_ref, coup_ref, piv_ref, col_ref, base_ref, v_ref, hxlo_ref, hxhi_ref, hylo_ref, hyhi_ref) = refs[:10]
    refs = refs[10:]
    if forward:
        u_ref, nv_ref, *edge_refs = refs
    else:
        nv_ref, *edge_refs = refs
    if forward:
        rhs_ref, old_ref = base_ref, None
    nz = base_ref.shape[1]
    ny, nx = base_ref.shape[2:]
    keep = colour if forward else colour
    lane = iota((ny, 128), 1)
    row = iota((ny, nx), 0)
    fxlo = meta_ref[1].astype(F32)
    fxhi = meta_ref[2].astype(F32)
    fylo = meta_ref[3].astype(F32)
    fyhi = meta_ref[4].astype(F32)
    hxlo = hxlo_ref[...] * fxlo
    hxhi = hxhi_ref[...] * fxhi
    if not final:
        zero_ends(nv_ref, nz)

    def step(z, edges):
        acc = [jnp.zeros((ny, nx), F32) for _ in range(3)]
        old = []
        for j in range(3):
            at = j * nz + z
            vc = v_ref[j, z + 1]
            old.append(vc)
            xm = pltpu.roll(vc, 1, 1)
            head = jnp.where(lane == 0, pltpu.roll(hxlo, (128 - at) % 128, 1), xm[:, :128])
            xm = jnp.concatenate([head, xm[:, 128:]], axis=1)
            xp = pltpu.roll(vc, nx - 1, 1)
            tail = jnp.where(lane == 127, pltpu.roll(hxhi, 127 - at, 1), xp[:, -128:])
            xp = jnp.concatenate([xp[:, :-128], tail], axis=1)
            ym = jnp.where(row == 0, hylo_ref[pl.ds(at, 1), :] * fylo, pltpu.roll(vc, 1, 0))
            yp = jnp.where(row == ny - 1, hyhi_ref[pl.ds(at, 1), :] * fyhi, pltpu.roll(vc, ny - 1, 0))
            zm = v_ref[j, z]
            zp = v_ref[j, z + 2]
            for i in range(3):
                t = coup_ref[0, i, j, z] * xm + coup_ref[1, i, j, z] * xp
                t = t + (coup_ref[2, i, j, z] * ym + coup_ref[3, i, j, z] * yp)
                t = t + (coup_ref[4, i, j, z] * zm + coup_ref[5, i, j, z] * zp)
                acc[i] = acc[i] + t
        chosen = col_ref[z] == colour
        base = [base_ref[j, z] for j in range(3)]
        if forward:
            cur = []
            for j in range(3):
                cur.append(base[j] - acc[j])
        else:
            cur = [base[j] - acc[j] for j in range(3)]
        new = []
        for i in range(3):
            p = piv_ref[i, 0, z] * cur[0] + piv_ref[i, 1, z] * cur[1] + piv_ref[i, 2, z] * cur[2]
            if forward:
                u_ref[i, z] = jnp.where(chosen, cur[i], base[i])
                keep_old = 0.0 if colour == 3 else old[i]
            else:
                keep_old = old[i]
            p = jnp.where(chosen, p, keep_old)
            if final:
                nv_ref[i, z] = p
            else:
                nv_ref[i, z + 1] = p
            new.append(p)
        if final:
            return edges
        return emit_edges(new, z, nz, edges, edge_refs[2], edge_refs[3])

    zero = jnp.zeros((ny, 128), F32)
    xlo, xhi = lax.fori_loop(0, nz, step, (zero, zero))
    if not final:
        edge_refs[0][...] = xlo
        edge_refs[1][...] = xhi


def halos(edges):
    xlo, xhi, ylo, yhi = edges
    nx = lax.axis_size("gx")
    ny = lax.axis_size("gy")
    up_y = [(i, (i + 1) % ny) for i in range(ny)]
    dn_y = [((i + 1) % ny, i) for i in range(ny)]
    up_x = [(i, (i + 1) % nx) for i in range(nx)]
    dn_x = [((i + 1) % nx, i) for i in range(nx)]
    hylo = lax.ppermute(yhi, "gy", up_y)
    hyhi = lax.ppermute(ylo, "gy", dn_y)
    hxlo = lax.ppermute(xhi, "gx", up_x)
    hxhi = lax.ppermute(xlo, "gx", dn_x)
    return hxlo, hxhi, hylo, hyhi


def prep_body(meta_ref, slot_ref, count_ref, cells_ref, wells_ref, segs_ref, kh_ref, rt_ref, e_ref, alive_ref, lo_ref):
    n = cells_ref.shape[1]
    wells = wells_ref[...]
    table = slot_ref[...]
    pick = (iota((table.shape[0], n), 0) == (wells >> 7)).astype(BF16)
    high = dot((table >> 7).astype(F32).astype(BF16), pick, ((0,), (0,)))
    low = dot((table & 127).astype(F32).astype(BF16), pick, ((0,), (0,)))
    slot = jnp.where(iota((128, n), 0) == (wells & 127), high * 128.0 + low, 0.0)
    slot = jnp.sum(slot, axis=0, keepdims=True).astype(jnp.int32)
    key = slot * 16 + segs_ref[...]
    lo_ref[...] = key & 127
    kh_ref[...] = (iota(kh_ref.shape, 0) == (key >> 7)).astype(F32).astype(BF16)
    rt_ref[...] = (iota(rt_ref.shape, 0) == (cells_ref[...] >> 8)).astype(F32).astype(BF16)
    a = iota(e_ref.shape, 0)
    b = iota(e_ref.shape, 1)
    same = ((a >> 4) == ((b & 127) >> 4)) & ((a & 15) == (b >> 7))
    e_ref[...] = same.astype(F32).astype(BF16)
    tile = meta_ref[0]
    own_slot = slot_ref[pl.ds(tile // 2, 1), :] - tile * 64
    own_count = count_ref[pl.ds(tile // 2, 1), :].astype(F32)
    left = jnp.where(iota((8, 128), 0) == (own_slot >> 3), own_count, 0.0).astype(BF16)
    right = ((iota((128, 128), 0) >> 4) == (own_slot & 7)).astype(F32).astype(BF16)
    counts = dot(left, right, ((1,), (1,)))
    alive_ref[...] = ((iota((8, 128), 1) & 15).astype(F32) < counts).astype(F32)


def terms_body(s_ref, rt_ref, kh_ref, lo_ref, cells_ref, gather_ref, out_ref):
    n = cells_ref.shape[1]
    rt = rt_ref[...]
    at_col = iota((256, n), 0) == (cells_ref[...] & 255)
    term = jnp.zeros((1, n), F32)
    for i in range(3):
        f = s_ref[i].reshape(256, 256)
        g = sum(dot(h, rt, ((0,), (0,))) for h in split3(f))
        v = jnp.sum(jnp.where(at_col, g, 0.0), axis=0, keepdims=True)
        term = term + gather_ref[pl.ds(i, 1), :] * v
    at_low = iota((128, n), 0) == lo_ref[...]
    stack = jnp.concatenate([jnp.where(at_low, h.astype(F32), 0.0).astype(BF16) for h in split3(term)], axis=0)
    sums = dot(kh_ref[...], stack, ((1,), (1,)))
    out_ref[...] = sums[:, :128] + sums[:, 128:256] + sums[:, 256:]


def solve_body(got_ref, q_ref, e_ref, alive_ref, out_ref):
    alive = alive_ref[...]
    totals = jnp.sum(got_ref[...], axis=0) * alive
    spread = sum(dot(h, e_ref[...], ((1,), (0,))) for h in split3(totals))
    values = jnp.zeros((8, 128), F32)
    for j in range(16):
        values = values + q_ref[j] * spread[:, j * 128 : (j + 1) * 128]
    values = values * alive
    out_ref[...] = jnp.broadcast_to(values[None], out_ref.shape)


def return_body(table_ref, s_ref, rt_ref, kh_ref, lo_ref, cells_ref, back_ref, out_ref):
    n = cells_ref.shape[1]
    kh = kh_ref[...]
    table = table_ref[...].reshape(1024, 128)
    g = sum(dot(h, kh, ((0,), (0,))) for h in split3(table))
    values = jnp.sum(jnp.where(iota((128, n), 0) == lo_ref[...], g, 0.0), axis=0, keepdims=True)
    at_col = iota((256, n), 0) == (cells_ref[...] & 255)
    rt = rt_ref[...]
    for i in range(3):
        w = back_ref[pl.ds(i, 1), :] * values
        change = sum(
            dot(rt, jnp.where(at_col, h.astype(F32), 0.0).astype(BF16), ((1,), (1,))) for h in split3(w)
        )
        out_ref[i] = s_ref[i] - change.reshape(32, 8, 256)


def shards(
    rhs,
    couplings,
    pivots,
    colours,
    perf_cells,
    perf_wells,
    perf_segments,
    perf_gather,
    perf_return,
    well_slot,
    seg_count,
    well_inverses,
):
    axes = ("gx", "gy")
    devices = lax.axis_size(axes)
    gx = lax.axis_index("gx")
    gy = lax.axis_index("gy")
    tile = lax.axis_index(axes)
    meta = jnp.stack(
        [
            tile,
            (gx > 0).astype(jnp.int32),
            (gx < lax.axis_size("gx") - 1).astype(jnp.int32),
            (gy > 0).astype(jnp.int32),
            (gy < lax.axis_size("gy") - 1).astype(jnp.int32),
        ]
    ).astype(jnp.int32)
    _, nz, ny, nx = rhs.shape
    field = ((3, nz + 2, ny, nx), F32)
    plain = ((3, nz, ny, nx), F32)
    edges = [((ny, 128), F32)] * 2 + [((3 * nz, nx), F32)] * 2
    n = perf_cells.shape[0]
    cells = perf_cells.reshape(1, n)

    kh, rt, spread, alive, low = call(
        prep_body,
        [((1024, n), BF16), ((256, n), BF16), ((128, 2048), BF16), ((8, 128), F32), ((1, n), jnp.int32)],
        [
            meta,
            well_slot.reshape(-1, 128),
            seg_count.reshape(-1, 128),
            cells,
            perf_wells.reshape(1, n),
            perf_segments.reshape(1, n),
        ],
        smem=1,
        name="prep",
    )
    q = well_inverses.reshape(8, 8, 16, 16).transpose(3, 0, 1, 2).reshape(16, 8, 128)

    v, *edge = call(first_body, [field] + edges, [rhs, pivots, colours], name="first")
    base = rhs
    for colour in (1, 2, 3):
        halo = halos(edge)
        base, v, *edge = call(
            lambda *r, c=colour: turn_body(c, True, False, *r),
            [plain, field] + edges,
            [meta, couplings, pivots, colours, base, v, *halo],
            smem=1,
            name=f"forward{colour}",
        )
    for colour in (2, 1, 0):
        halo = halos(edge)
        final = colour == 0
        v, *edge = call(
            lambda *r, c=colour, f=final: turn_body(c, False, f, *r),
            [plain] if final else [field] + edges,
            [meta, couplings, pivots, colours, base, v, *halo],
            smem=1,
            name=f"backward{colour}",
        )
    (totals,) = call(
        terms_body, [((1024, 128), F32)], [v, rt, kh, low, cells, perf_gather], name="terms", limit=24 << 20
    )
    got = lax.all_to_all(totals.reshape(devices, 8, 128), axes, 0, 0, tiled=True)
    (values,) = call(solve_body, [((devices, 8, 128), F32)], [got, q, spread, alive], name="solve")
    table = lax.all_to_all(values, axes, 0, 0, tiled=True)
    return pl.pallas_call(
        return_body,
        out_shape=jax.ShapeDtypeStruct(rhs.shape, F32),
        in_specs=[VMEM_SPEC] * 7,
        out_specs=VMEM_SPEC,
        compiler_params=pltpu.CompilerParams(vmem_limit_bytes=24 << 20),
        name="back",
    )(*[in_vmem(x) for x in (table, v, rt, kh, low, cells, perf_return)])


def solution(mesh):
    return jax.shard_map(
        shards,
        mesh=mesh,
        in_specs=(
            P(None, None, "gy", "gx"),
            P(None, None, None, None, "gy", "gx"),
            P(None, None, None, "gy", "gx"),
            P(None, "gy", "gx"),
            P(("gx", "gy")),
            P(("gx", "gy")),
            P(("gx", "gy")),
            P(None, ("gx", "gy")),
            P(None, ("gx", "gy")),
            P(),
            P(),
            P(("gx", "gy"), None, None),
        ),
        out_specs=P(None, None, "gy", "gx"),
        check_vma=False,
    )
```

```python
import jax
import jax.numpy as jnp
from jax import lax
from jax.experimental import pallas as pl
from jax.experimental.pallas import tpu as pltpu
from jax.sharding import PartitionSpec as P

F32 = jnp.float32
BF16 = jnp.bfloat16
UNROLL = 8
PARTS = 4
VMEM_SPEC = pl.BlockSpec(memory_space=pltpu.VMEM)
SMEM_SPEC = pl.BlockSpec(memory_space=pltpu.SMEM)


def iota(shape, dim):
    return lax.broadcasted_iota(jnp.int32, shape, dim)


def split3(x):
    a = x.astype(BF16)
    r = x - a.astype(F32)
    b = r.astype(BF16)
    c = (r - b.astype(F32)).astype(BF16)
    return a, b, c


def dot(a, b, dims):
    return lax.dot_general(a, b, (dims, ((), ())), preferred_element_type=F32)


def in_vmem(x):
    return pltpu.with_memory_space_constraint(x, pltpu.VMEM)


def call(body, outs, ins, smem=0, hbm=(), scratch=(), name=None, limit=None):
    specs, args = [], []
    for k, x in enumerate(ins):
        if k < smem:
            specs.append(SMEM_SPEC)
        elif k in hbm:
            specs.append(pl.BlockSpec(memory_space=pltpu.HBM))
            x = pltpu.with_memory_space_constraint(x, pltpu.HBM)
        else:
            specs.append(VMEM_SPEC)
            x = in_vmem(x)
        args.append(x)
    return pl.pallas_call(
        body,
        out_shape=tuple(pltpu.VMEM(s, d) for s, d in outs),
        in_specs=specs,
        out_specs=tuple(VMEM_SPEC for _ in outs),
        scratch_shapes=list(scratch),
        compiler_params=pltpu.CompilerParams(vmem_limit_bytes=limit or (8 << 20)),
        name=name,
    )(*args)


def emit_edges(new, z, nz, edges, y_odd, ya_ref, yb_ref):
    xlo, xhi = edges
    lane = iota((8, 128), 1)
    for j in range(3):
        at = j * nz + z
        xlo = jnp.where(lane == at, pltpu.roll(new[j][:, :128], at, 1), xlo)
        xhi = jnp.where(lane == at, pltpu.roll(new[j][:, -128:], (at + 1) % 128, 1), xhi)
        first, last = new[j][0:1, :], new[j][-1:, :]
        ya_ref[pl.ds(at, 1), :] = jnp.where(y_odd, first, last)
        yb_ref[pl.ds(at, 1), :] = jnp.where(y_odd, last, first)
    return xlo, xhi


def store_columns(x_odd, edges, xa_ref, xb_ref):
    xlo, xhi = edges
    xa_ref[...] = jnp.where(x_odd, xlo, xhi)
    xb_ref[...] = jnp.where(x_odd, xhi, xlo)


def zero_ends(ref, nz):
    zero = jnp.zeros(ref.shape[2:], F32)
    for j in range(3):
        ref[j, 0] = zero
        ref[j, nz + 1] = zero


def chunk_copies(pairs, sems, part, size, axes):
    out = []
    for k, ((src, dst), axis) in enumerate(zip(pairs, axes)):
        at = (slice(None),) * axis + (pl.ds(part * size, size),)
        out.append(pltpu.make_async_copy(src.at[at], dst.at[at], sems.at[k, part]))
    return out


def first_body(meta_ref, rhs_hbm, piv_hbm, col_hbm, rhs_ref, piv_ref, col_ref, v_ref, xa_ref, xb_ref, ya_ref, yb_ref, sems):
    nz = rhs_ref.shape[1]
    size = nz // PARTS
    pairs = [(rhs_hbm, rhs_ref), (piv_hbm, piv_ref), (col_hbm, col_ref)]
    for part in range(PARTS):
        for c in chunk_copies(pairs, sems, part, size, (1, 2, 0)):
            c.start()
    zero_ends(v_ref, nz)
    x_odd = meta_ref[5] > 0
    y_odd = meta_ref[6] > 0

    def step(z, edges):
        rhs = [rhs_ref[j, z] for j in range(3)]
        chosen = col_ref[z] == 0
        new = []
        for i in range(3):
            p = piv_ref[i, 0, z] * rhs[0] + piv_ref[i, 1, z] * rhs[1] + piv_ref[i, 2, z] * rhs[2]
            p = jnp.where(chosen, p, 0.0)
            v_ref[i, z + 1] = p
            new.append(p)
        return emit_edges(new, z, nz, edges, y_odd, ya_ref, yb_ref)

    def block(part, edges):
        for c in chunk_copies(pairs, sems, part, size, (1, 2, 0)):
            c.wait()
        return lax.fori_loop(0, size, lambda k, e: step(part * size + k, e), edges, unroll=UNROLL)

    zero = jnp.zeros((8, 128), F32)
    edges = lax.fori_loop(0, PARTS, block, (zero, zero))
    store_columns(x_odd, edges, xa_ref, xb_ref)


def turn_body(colour, forward, final, load, *refs):
    (meta_ref, coup_ref, piv_ref, col_ref, base_ref, v_ref, hxa_ref, hxb_ref, hya_ref, hyb_ref) = refs[:10]
    refs = list(refs[10:])
    if load:
        sems = refs.pop()
        coup_hbm, coup_ref = coup_ref, refs.pop(0)
    u_ref = refs.pop(0) if forward else None
    nv_ref, *edge_refs = refs
    nz = base_ref.shape[1]
    ny, nx = base_ref.shape[2:]
    size = nz // PARTS
    pairs = [(coup_hbm, coup_ref)] if load else []
    if load:
        for part in range(PARTS):
            for c in chunk_copies(pairs, sems, part, size, (3,)):
                c.start()
    lane = iota((ny, 128), 1)
    row = iota((ny, nx), 0)
    x_odd = meta_ref[5] > 0
    y_odd = meta_ref[6] > 0
    has = [meta_ref[k] > 0 for k in range(1, 5)]
    hxa, hxb = hxa_ref[...], hxb_ref[...]
    hxlo = jnp.where(has[0], jnp.where(x_odd, hxa, hxb), 0.0)
    hxhi = jnp.where(has[1], jnp.where(x_odd, hxb, hxa), 0.0)
    if not final:
        zero_ends(nv_ref, nz)

    def step(z, edges):
        acc = [jnp.zeros((ny, nx), F32) for _ in range(3)]
        old = []
        for j in range(3):
            at = j * nz + z
            vc = v_ref[j, z + 1]
            old.append(vc)
            xm = pltpu.roll(vc, 1, 1)
            head = jnp.where(lane == 0, pltpu.roll(hxlo, (128 - at) % 128, 1), xm[:, :128])
            xm = jnp.concatenate([head, xm[:, 128:]], axis=1)
            xp = pltpu.roll(vc, nx - 1, 1)
            tail = jnp.where(lane == 127, pltpu.roll(hxhi, 127 - at, 1), xp[:, -128:])
            xp = jnp.concatenate([xp[:, :-128], tail], axis=1)
            ha, hb = hya_ref[pl.ds(at, 1), :], hyb_ref[pl.ds(at, 1), :]
            hylo = jnp.where(has[2], jnp.where(y_odd, ha, hb), 0.0)
            hyhi = jnp.where(has[3], jnp.where(y_odd, hb, ha), 0.0)
            ym = jnp.where(row == 0, hylo, pltpu.roll(vc, 1, 0))
            yp = jnp.where(row == ny - 1, hyhi, pltpu.roll(vc, ny - 1, 0))
            zm = v_ref[j, z]
            zp = v_ref[j, z + 2]
            for i in range(3):
                t = coup_ref[0, i, j, z] * xm + coup_ref[1, i, j, z] * xp
                t = t + (coup_ref[2, i, j, z] * ym + coup_ref[3, i, j, z] * yp)
                t = t + (coup_ref[4, i, j, z] * zm + coup_ref[5, i, j, z] * zp)
                acc[i] = acc[i] + t
        chosen = col_ref[z] == colour
        base = [base_ref[j, z] for j in range(3)]
        cur = [base[j] - acc[j] for j in range(3)]
        new = []
        for i in range(3):
            p = piv_ref[i, 0, z] * cur[0] + piv_ref[i, 1, z] * cur[1] + piv_ref[i, 2, z] * cur[2]
            if forward:
                u_ref[i, z] = jnp.where(chosen, cur[i], base[i])
                keep_old = 0.0 if colour == 3 else old[i]
            else:
                keep_old = old[i]
            p = jnp.where(chosen, p, keep_old)
            if final:
                nv_ref[i, z] = p
            else:
                nv_ref[i, z + 1] = p
            new.append(p)
        if final:
            return edges
        return emit_edges(new, z, nz, edges, y_odd, edge_refs[2], edge_refs[3])

    def block(part, edges):
        for c in chunk_copies(pairs, sems, part, size, (3,)):
            c.wait()
        return lax.fori_loop(0, size, lambda k, e: step(part * size + k, e), edges, unroll=UNROLL)

    zero = jnp.zeros((ny, 128), F32)
    if load:
        edges = lax.fori_loop(0, PARTS, block, (zero, zero))
    else:
        edges = lax.fori_loop(0, nz, step, (zero, zero), unroll=UNROLL)
    if not final:
        store_columns(x_odd, edges, edge_refs[0], edge_refs[1])


def swaps(size, odd):
    out = []
    for i in range(odd, size + odd, 2):
        a, b = i % size, (i + 1) % size
        out += [(a, b), (b, a)]
    return out


def halos(edges):
    xa, xb, ya, yb = edges
    nx = lax.axis_size("gx")
    ny = lax.axis_size("gy")
    hxb = lax.ppermute(xb, "gx", swaps(nx, 1))
    hyb = lax.ppermute(yb, "gy", swaps(ny, 1))
    hxa = lax.ppermute(xa, "gx", swaps(nx, 0))
    hya = lax.ppermute(ya, "gy", swaps(ny, 0))
    return hxa, hxb, hya, hyb


def prep_body(meta_ref, slot_ref, count_ref, cells_ref, wells_ref, segs_ref, kh_ref, rt_ref, alive_ref, lo_ref):
    n = cells_ref.shape[1]
    wells = wells_ref[...]
    table = slot_ref[...]
    pick = (iota((table.shape[0], n), 0) == (wells >> 7)).astype(BF16)
    high = dot((table >> 7).astype(F32).astype(BF16), pick, ((0,), (0,)))
    low = dot((table & 127).astype(F32).astype(BF16), pick, ((0,), (0,)))
    slot = jnp.where(iota((128, n), 0) == (wells & 127), high * 128.0 + low, 0.0)
    slot = jnp.sum(slot, axis=0, keepdims=True).astype(jnp.int32)
    segs = segs_ref[...]
    owner = slot >> 6
    tile = meta_ref[0]
    rows = ((owner ^ tile) & 1) * 512 + (owner >> 1) * 8 + (segs & 7)
    lo_ref[...] = (segs >> 3) * 64 + (slot & 63)
    kh_ref[...] = (iota(kh_ref.shape, 0) == rows).astype(F32).astype(BF16)
    rt_ref[...] = (iota(rt_ref.shape, 0) == (cells_ref[...] >> 8)).astype(F32).astype(BF16)
    own_slot = slot_ref[pl.ds(tile // 2, 1), :] - tile * 64
    own_count = jnp.broadcast_to(count_ref[pl.ds(tile // 2, 1), :].astype(F32), (8, 128)).astype(BF16)
    match = (iota((128, 128), 0) == own_slot).astype(F32).astype(BF16)
    counts = dot(own_count, match, ((1,), (1,)))
    alive_ref[0:8] = (iota((8, 128), 0).astype(F32) < counts).astype(F32)
    alive_ref[8:16] = ((iota((8, 128), 0) + 8).astype(F32) < counts).astype(F32)


def terms_body(s_ref, rt_ref, kh_ref, lo_ref, cells_ref, gather_ref, mine_ref, other_ref):
    n = cells_ref.shape[1]
    rt = rt_ref[...]
    at_col = iota((256, n), 0) == (cells_ref[...] & 255)
    term = jnp.zeros((1, n), F32)
    for i in range(3):
        f = s_ref[i].reshape(256, 256)
        g = sum(dot(h, rt, ((0,), (0,))) for h in split3(f))
        v = jnp.sum(jnp.where(at_col, g, 0.0), axis=0, keepdims=True)
        term = term + gather_ref[pl.ds(i, 1), :] * v
    at_low = iota((128, n), 0) == lo_ref[...]
    stack = jnp.concatenate([jnp.where(at_low, h.astype(F32), 0.0).astype(BF16) for h in split3(term)], axis=0)
    sums = dot(kh_ref[...], stack, ((1,), (1,)))
    sums = sums[:, :128] + sums[:, 128:256] + sums[:, 256:]
    mine_ref[...] = sums[:512]
    other_ref[...] = sums[512:]


def solve_body(got_ref, inv_ref, alive_ref, out_ref):
    alive = alive_ref[:, :64]
    totals = jnp.sum(got_ref[...], axis=0)
    totals = jnp.concatenate([totals[:, :64], totals[:, 64:]], axis=0) * alive
    rows = [jnp.sum(inv_ref[i] * totals, axis=0, keepdims=True) for i in range(16)]
    values = jnp.concatenate(rows, axis=0) * alive
    values = jnp.concatenate([values[:8], values[8:]], axis=1)
    out_ref[...] = jnp.broadcast_to(values[None], out_ref.shape)


def return_body(mine_ref, other_ref, s_ref, rt_ref, kh_ref, lo_ref, cells_ref, back_ref, out_ref):
    n = cells_ref.shape[1]
    g = sum(dot(h, kh_ref[0:512], ((0,), (0,))) for h in split3(mine_ref[...]))
    g = g + sum(dot(h, kh_ref[512:1024], ((0,), (0,))) for h in split3(other_ref[...]))
    values = jnp.sum(jnp.where(iota((128, n), 0) == lo_ref[...], g, 0.0), axis=0, keepdims=True)
    at_col = iota((256, n), 0) == (cells_ref[...] & 255)
    rt = rt_ref[...]
    for i in range(3):
        w = back_ref[pl.ds(i, 1), :] * values
        change = sum(
            dot(rt, jnp.where(at_col, h.astype(F32), 0.0).astype(BF16), ((1,), (1,))) for h in split3(w)
        )
        out_ref[i] = s_ref[i] - change.reshape(32, 8, 256)


def shards(
    rhs,
    couplings,
    pivots,
    colours,
    perf_cells,
    perf_wells,
    perf_segments,
    perf_gather,
    perf_return,
    well_slot,
    seg_count,
    well_inverses,
):
    axes = ("gx", "gy")
    devices = lax.axis_size(axes)
    gx = lax.axis_index("gx")
    gy = lax.axis_index("gy")
    tile = lax.axis_index(axes)
    meta = jnp.stack(
        [
            tile,
            gx > 0,
            gx < lax.axis_size("gx") - 1,
            gy > 0,
            gy < lax.axis_size("gy") - 1,
            gx % 2,
            gy % 2,
        ]
    ).astype(jnp.int32)
    _, nz, ny, nx = rhs.shape
    field = ((3, nz + 2, ny, nx), F32)
    plain = ((3, nz, ny, nx), F32)
    edges = [((ny, 128), F32)] * 2 + [((3 * nz, nx), F32)] * 2
    n = perf_cells.shape[0]
    cells = perf_cells.reshape(1, n)

    rhs, pivots, colours, v, *edge = call(
        first_body,
        [plain, (pivots.shape, F32), (colours.shape, jnp.int32), field] + edges,
        [meta, rhs, pivots, colours],
        smem=1,
        hbm=(1, 2, 3),
        scratch=[pltpu.SemaphoreType.DMA((3, PARTS))],
        name="first",
    )
    base = rhs
    for colour in (1, 2, 3):
        halo = halos(edge)
        load = colour == 1
        got = call(
            lambda *r, c=colour, l=load: turn_body(c, True, False, l, *r),
            ([(couplings.shape, F32)] if load else []) + [plain, field] + edges,
            [meta, couplings, pivots, colours, base, v, *halo],
            smem=1,
            hbm=(1,) if load else (),
            scratch=[pltpu.SemaphoreType.DMA((1, PARTS))] if load else [],
            name=f"forward{colour}",
        )
        if load:
            couplings, *got = got
        base, v, *edge = got
    kh, rt, alive, low = call(
        prep_body,
        [((1024, n), BF16), ((256, n), BF16), ((16, 128), F32), ((1, n), jnp.int32)],
        [
            meta,
            well_slot.reshape(-1, 128),
            seg_count.reshape(-1, 128),
            cells,
            perf_wells.reshape(1, n),
            perf_segments.reshape(1, n),
        ],
        smem=1,
        name="prep",
    )
    for colour in (2, 1, 0):
        halo = halos(edge)
        final = colour == 0
        v, *edge = call(
            lambda *r, c=colour, f=final: turn_body(c, False, f, False, *r),
            [plain] if final else [field] + edges,
            [meta, couplings, pivots, colours, base, v, *halo],
            smem=1,
            name=f"backward{colour}",
        )
    pairs = swaps(lax.axis_size("gy"), 0)
    cores = [[d for d in range(devices) if d % 2 == core] for core in range(2)]
    mine, other = call(
        terms_body, [((512, 128), F32)] * 2, [v, rt, kh, low, cells, perf_gather], name="terms", limit=24 << 20
    )
    mine = mine + lax.ppermute(other, "gy", pairs)
    got = lax.all_to_all(mine.reshape(64, 8, 128), axes, 0, 0, axis_index_groups=cores, tiled=True)
    (values,) = call(
        solve_body, [((64, 8, 128), F32)], [got, well_inverses.transpose(1, 2, 0), alive], name="solve"
    )
    mine = lax.all_to_all(values, axes, 0, 0, axis_index_groups=cores, tiled=True).reshape(512, 128)
    other = lax.ppermute(mine, "gy", pairs)
    return pl.pallas_call(
        return_body,
        out_shape=jax.ShapeDtypeStruct(plain[0], F32),
        in_specs=[VMEM_SPEC] * 8,
        out_specs=VMEM_SPEC,
        compiler_params=pltpu.CompilerParams(vmem_limit_bytes=24 << 20),
        name="back",
    )(*[in_vmem(x) for x in (mine, other, v, rt, kh, low, cells, perf_return)])


def solution(mesh):
    return jax.shard_map(
        shards,
        mesh=mesh,
        in_specs=(
            P(None, None, "gy", "gx"),
            P(None, None, None, None, "gy", "gx"),
            P(None, None, None, "gy", "gx"),
            P(None, "gy", "gx"),
            P(("gx", "gy")),
            P(("gx", "gy")),
            P(("gx", "gy")),
            P(None, ("gx", "gy")),
            P(None, ("gx", "gy")),
            P(),
            P(),
            P(("gx", "gy"), None, None),
        ),
        out_specs=P(None, None, "gy", "gx"),
        check_vma=False,
    )
```

```python
import jax
import jax.numpy as jnp
from jax import lax
from jax.experimental import pallas as pl
from jax.experimental.pallas import tpu as pltpu
from jax.sharding import PartitionSpec as P

F32 = jnp.float32
BF16 = jnp.bfloat16
UNROLL = 8
PARTS = 4
VMEM_SPEC = pl.BlockSpec(memory_space=pltpu.VMEM)
SMEM_SPEC = pl.BlockSpec(memory_space=pltpu.SMEM)


def iota(shape, dim):
    return lax.broadcasted_iota(jnp.int32, shape, dim)


def split(x):
    a = x.astype(BF16)
    return a, (x - a.astype(F32)).astype(BF16)


def dot(a, b, dims):
    return lax.dot_general(a, b, (dims, ((), ())), preferred_element_type=F32)


def in_vmem(x):
    return pltpu.with_memory_space_constraint(x, pltpu.VMEM)


def call(body, outs, ins, smem=0, hbm=(), scratch=(), name=None, limit=None, cost=None, alias=None):
    specs, args = [], []
    for k, x in enumerate(ins):
        if k < smem:
            specs.append(SMEM_SPEC)
        elif k in hbm:
            specs.append(pl.BlockSpec(memory_space=pltpu.HBM))
            x = pltpu.with_memory_space_constraint(x, pltpu.HBM)
        else:
            specs.append(VMEM_SPEC)
            x = in_vmem(x)
        args.append(x)
    return pl.pallas_call(
        body,
        out_shape=tuple(pltpu.VMEM(s, d) for s, d in outs),
        in_specs=specs,
        out_specs=tuple(VMEM_SPEC for _ in outs),
        scratch_shapes=list(scratch),
        compiler_params=pltpu.CompilerParams(vmem_limit_bytes=limit or (8 << 20)),
        cost_estimate=cost,
        input_output_aliases=alias or {},
        name=name,
    )(*args)


def emit_edges(new, z, nz, edges, ylo_ref, yhi_ref):
    xlo, xhi = edges
    lane = iota((8, 128), 1)
    for j in range(3):
        at = j * nz + z
        xlo = jnp.where(lane == at, pltpu.roll(new[j][:, :128], at, 1), xlo)
        xhi = jnp.where(lane == at, pltpu.roll(new[j][:, -128:], (at + 1) % 128, 1), xhi)
        ylo_ref[pl.ds(at, 1), :] = new[j][0:1, :]
        yhi_ref[pl.ds(at, 1), :] = new[j][-1:, :]
    return xlo, xhi


def store_edges(meta_ref, columns, ylo_ref, yhi_ref, xa_ref, xb_ref, ya_ref, yb_ref):
    x_odd = meta_ref[5] > 0
    y_odd = meta_ref[6] > 0
    xlo, xhi = columns
    xa_ref[...] = jnp.where(x_odd, xlo, xhi)
    xb_ref[...] = jnp.where(x_odd, xhi, xlo)
    ylo, yhi = ylo_ref[...], yhi_ref[...]
    ya_ref[...] = jnp.where(y_odd, ylo, yhi)
    yb_ref[...] = jnp.where(y_odd, yhi, ylo)


def zero_ends(ref, nz):
    zero = jnp.zeros(ref.shape[2:], F32)
    for j in range(3):
        ref[j, 0] = zero
        ref[j, nz + 1] = zero


def chunk_copies(pairs, sems, part, size, axes):
    out = []
    for k, ((src, dst), axis) in enumerate(zip(pairs, axes)):
        at = (slice(None),) * axis + (pl.ds(part * size, size),)
        out.append(pltpu.make_async_copy(src.at[at], dst.at[at], sems.at[k, part]))
    return out


def first_body(meta_ref, rhs_hbm, piv_hbm, col_hbm, rhs_ref, piv_ref, col_ref, v_ref, xa_ref, xb_ref, ya_ref, yb_ref, ylo_ref, yhi_ref, sems):
    nz = rhs_ref.shape[1]
    size = nz // PARTS
    pairs = [(rhs_hbm, rhs_ref), (piv_hbm, piv_ref), (col_hbm, col_ref)]
    for part in range(PARTS):
        for c in chunk_copies(pairs, sems, part, size, (1, 2, 0)):
            c.start()
    zero_ends(v_ref, nz)

    def step(z, edges):
        rhs = [rhs_ref[j, z] for j in range(3)]
        chosen = col_ref[z] == 0
        new = []
        for i in range(3):
            p = piv_ref[i, 0, z] * rhs[0] + piv_ref[i, 1, z] * rhs[1] + piv_ref[i, 2, z] * rhs[2]
            p = jnp.where(chosen, p, 0.0)
            v_ref[i, z + 1] = p
            new.append(p)
        return emit_edges(new, z, nz, edges, ylo_ref, yhi_ref)

    def block(part, edges):
        for c in chunk_copies(pairs, sems, part, size, (1, 2, 0)):
            c.wait()
        return lax.fori_loop(0, size, lambda k, e: step(part * size + k, e), edges, unroll=UNROLL)

    zero = jnp.zeros((8, 128), F32)
    edges = lax.fori_loop(0, PARTS, block, (zero, zero))
    store_edges(meta_ref, edges, ylo_ref, yhi_ref, xa_ref, xb_ref, ya_ref, yb_ref)


def turn_body(colour, forward, final, load, *refs):
    (meta_ref, coup_ref, piv_ref, col_ref, base_ref, v_ref, hxa_ref, hxb_ref, hya_ref, hyb_ref) = refs[:10]
    refs = list(refs[10:])
    if load:
        sems = refs.pop()
        prep_in, refs = refs[:5], refs[5:]
        coup_hbm, coup_ref = coup_ref, refs.pop(0)
        prep_out, refs = refs[:4], refs[4:]
    refs, (hylo_ref, hyhi_ref, ylo_ref, yhi_ref) = refs[:-4], refs[-4:]
    u_ref = refs.pop(0) if forward else None
    nv_ref, *edge_refs = refs
    nz = base_ref.shape[1]
    ny, nx = base_ref.shape[2:]
    size = nz // PARTS
    pairs = [(coup_hbm, coup_ref)] if load else []
    if load:
        for part in range(PARTS):
            for c in chunk_copies(pairs, sems, part, size, (3,)):
                c.start()
        prep_body(meta_ref, *prep_in, *prep_out)
    lane = iota((ny, 128), 1)
    row = iota((ny, nx), 0)
    x_odd = meta_ref[5] > 0
    y_odd = meta_ref[6] > 0
    has = [meta_ref[k] > 0 for k in range(1, 5)]
    hxa, hxb = hxa_ref[...], hxb_ref[...]
    hxlo = jnp.where(has[0], jnp.where(x_odd, hxa, hxb), 0.0)
    hxhi = jnp.where(has[1], jnp.where(x_odd, hxb, hxa), 0.0)
    hya, hyb = hya_ref[...], hyb_ref[...]
    hylo_ref[...] = jnp.where(has[2], jnp.where(y_odd, hya, hyb), 0.0)
    hyhi_ref[...] = jnp.where(has[3], jnp.where(y_odd, hyb, hya), 0.0)
    if not final:
        zero_ends(nv_ref, nz)

    def step(z, edges):
        acc = [jnp.zeros((ny, nx), F32) for _ in range(3)]
        old = []
        for j in range(3):
            at = j * nz + z
            vc = v_ref[j, z + 1]
            old.append(vc)
            xm = pltpu.roll(vc, 1, 1)
            head = jnp.where(lane == 0, pltpu.roll(hxlo, (128 - at) % 128, 1), xm[:, :128])
            xm = jnp.concatenate([head, xm[:, 128:]], axis=1)
            xp = pltpu.roll(vc, nx - 1, 1)
            tail = jnp.where(lane == 127, pltpu.roll(hxhi, 127 - at, 1), xp[:, -128:])
            xp = jnp.concatenate([xp[:, :-128], tail], axis=1)
            ym = jnp.where(row == 0, hylo_ref[pl.ds(at, 1), :], pltpu.roll(vc, 1, 0))
            yp = jnp.where(row == ny - 1, hyhi_ref[pl.ds(at, 1), :], pltpu.roll(vc, ny - 1, 0))
            zm = v_ref[j, z]
            zp = v_ref[j, z + 2]
            for i in range(3):
                t = coup_ref[0, i, j, z] * xm + coup_ref[1, i, j, z] * xp
                t = t + (coup_ref[2, i, j, z] * ym + coup_ref[3, i, j, z] * yp)
                t = t + (coup_ref[4, i, j, z] * zm + coup_ref[5, i, j, z] * zp)
                acc[i] = acc[i] + t
        chosen = col_ref[z] == colour
        base = [base_ref[j, z] for j in range(3)]
        cur = [base[j] - acc[j] for j in range(3)]
        new = []
        for i in range(3):
            p = piv_ref[i, 0, z] * cur[0] + piv_ref[i, 1, z] * cur[1] + piv_ref[i, 2, z] * cur[2]
            if forward:
                u_ref[i, z] = jnp.where(chosen, cur[i], base[i])
                keep_old = 0.0 if colour == 3 else old[i]
            else:
                keep_old = old[i]
            p = jnp.where(chosen, p, keep_old)
            if final:
                nv_ref[i, z] = p
            else:
                nv_ref[i, z + 1] = p
            new.append(p)
        if final:
            return edges
        return emit_edges(new, z, nz, edges, ylo_ref, yhi_ref)

    def block(part, edges):
        for c in chunk_copies(pairs, sems, part, size, (3,)):
            c.wait()
        return lax.fori_loop(0, size, lambda k, e: step(part * size + k, e), edges, unroll=UNROLL)

    zero = jnp.zeros((ny, 128), F32)
    if load:
        edges = lax.fori_loop(0, PARTS, block, (zero, zero))
    else:
        edges = lax.fori_loop(0, nz, step, (zero, zero), unroll=UNROLL)
    if not final:
        store_edges(meta_ref, edges, ylo_ref, yhi_ref, *edge_refs)


def swaps(size, odd):
    out = []
    for i in range(odd, size + odd, 2):
        a, b = i % size, (i + 1) % size
        out += [(a, b), (b, a)]
    return out


def halos(edges):
    xa, xb, ya, yb = edges
    nx = lax.axis_size("gx")
    ny = lax.axis_size("gy")
    hxb = lax.ppermute(xb, "gx", swaps(nx, 1))
    hyb = lax.ppermute(yb, "gy", swaps(ny, 1))
    hxa = lax.ppermute(xa, "gx", swaps(nx, 0))
    hya = lax.ppermute(ya, "gy", swaps(ny, 0))
    return hxa, hxb, hya, hyb


def prep_body(meta_ref, slot_ref, count_ref, cells_ref, wells_ref, segs_ref, kh_ref, rt_ref, alive_ref, lo_ref):
    n = cells_ref.shape[1]
    wells = wells_ref[...]
    table = slot_ref[...]
    pick = (iota((table.shape[0], n), 0) == (wells >> 7)).astype(BF16)
    high = dot((table >> 7).astype(F32).astype(BF16), pick, ((0,), (0,)))
    low = dot((table & 127).astype(F32).astype(BF16), pick, ((0,), (0,)))
    slot = jnp.where(iota((128, n), 0) == (wells & 127), high * 128.0 + low, 0.0)
    slot = jnp.sum(slot, axis=0, keepdims=True).astype(jnp.int32)
    segs = segs_ref[...]
    owner = slot >> 6
    tile = meta_ref[0]
    rows = ((owner ^ tile) & 1) * 512 + (owner >> 1) * 8 + (segs & 7)
    lo_ref[...] = (segs >> 3) * 64 + (slot & 63)
    kh_ref[...] = (iota(kh_ref.shape, 0) == rows).astype(F32).astype(BF16)
    rt_ref[...] = (iota(rt_ref.shape, 0) == (cells_ref[...] >> 8)).astype(F32).astype(BF16)
    own_slot = slot_ref[pl.ds(tile // 2, 1), :] - tile * 64
    own_count = jnp.broadcast_to(count_ref[pl.ds(tile // 2, 1), :].astype(F32), (8, 128)).astype(BF16)
    match = (iota((128, 128), 0) == own_slot).astype(F32).astype(BF16)
    counts = dot(own_count, match, ((1,), (1,)))
    alive_ref[0:8] = (iota((8, 128), 0).astype(F32) < counts).astype(F32)
    alive_ref[8:16] = ((iota((8, 128), 0) + 8).astype(F32) < counts).astype(F32)


def terms_body(s_ref, rt_ref, kh_ref, lo_ref, cells_ref, gather_ref, mine_ref, other_ref):
    n = cells_ref.shape[1]
    rt = rt_ref[...]
    at_col = iota((256, n), 0) == (cells_ref[...] & 255)
    term = jnp.zeros((1, n), F32)
    for i in range(3):
        f = s_ref[i].reshape(256, 256)
        g = sum(dot(h, rt, ((0,), (0,))) for h in split(f))
        v = jnp.sum(jnp.where(at_col, g, 0.0), axis=0, keepdims=True)
        term = term + gather_ref[pl.ds(i, 1), :] * v
    at_low = iota((128, n), 0) == lo_ref[...]
    stack = jnp.concatenate([jnp.where(at_low, h.astype(F32), 0.0).astype(BF16) for h in split(term)], axis=0)
    sums = dot(kh_ref[...], stack, ((1,), (1,)))
    sums = sums[:, :128] + sums[:, 128:]
    mine_ref[...] = sums[:512]
    other_ref[...] = sums[512:]


def solve_body(got_ref, inv_ref, alive_ref, out_ref):
    alive = alive_ref[:, :64]
    totals = jnp.sum(got_ref[...], axis=0)
    totals = jnp.concatenate([totals[:, :64], totals[:, 64:]], axis=0) * alive
    rows = [jnp.sum(inv_ref[i] * totals, axis=0, keepdims=True) for i in range(16)]
    values = jnp.concatenate(rows, axis=0) * alive
    values = jnp.concatenate([values[:8], values[8:]], axis=1)
    out_ref[...] = jnp.broadcast_to(values[None], out_ref.shape)


def return_body(mine_ref, other_ref, s_ref, rt_ref, kh_ref, lo_ref, cells_ref, back_ref, out_ref):
    n = cells_ref.shape[1]
    g = sum(dot(h, kh_ref[0:512], ((0,), (0,))) for h in split(mine_ref[...]))
    g = g + sum(dot(h, kh_ref[512:1024], ((0,), (0,))) for h in split(other_ref[...]))
    values = jnp.sum(jnp.where(iota((128, n), 0) == lo_ref[...], g, 0.0), axis=0, keepdims=True)
    at_col = iota((256, n), 0) == (cells_ref[...] & 255)
    rt = rt_ref[...]
    for i in range(3):
        w = back_ref[pl.ds(i, 1), :] * values
        change = sum(
            dot(rt, jnp.where(at_col, h.astype(F32), 0.0).astype(BF16), ((1,), (1,))) for h in split(w)
        )
        out_ref[i] = s_ref[i] - change.reshape(32, 8, 256)


def shards(
    rhs,
    couplings,
    pivots,
    colours,
    perf_cells,
    perf_wells,
    perf_segments,
    perf_gather,
    perf_return,
    well_slot,
    seg_count,
    well_inverses,
):
    axes = ("gx", "gy")
    devices = lax.axis_size(axes)
    gx = lax.axis_index("gx")
    gy = lax.axis_index("gy")
    tile = lax.axis_index(axes)
    meta = jnp.stack(
        [
            tile,
            gx > 0,
            gx < lax.axis_size("gx") - 1,
            gy > 0,
            gy < lax.axis_size("gy") - 1,
            gx % 2,
            gy % 2,
        ]
    ).astype(jnp.int32)
    _, nz, ny, nx = rhs.shape
    field = ((3, nz + 2, ny, nx), F32)
    plain = ((3, nz, ny, nx), F32)
    edges = [((ny, 128), F32)] * 2 + [((3 * nz, nx), F32)] * 2
    n = perf_cells.shape[0]
    cells = perf_cells.reshape(1, n)
    rows = [pltpu.VMEM((3 * nz, nx), F32)] * 4
    prep_ins = [
        well_slot.reshape(-1, 128),
        seg_count.reshape(-1, 128),
        cells,
        perf_wells.reshape(1, n),
        perf_segments.reshape(1, n),
    ]
    prep_outs = [((1024, n), BF16), ((256, n), BF16), ((16, 128), F32), ((1, n), jnp.int32)]

    rhs, pivots, colours, v, *edge = call(
        first_body,
        [plain, (pivots.shape, F32), (colours.shape, jnp.int32), field] + edges,
        [meta, rhs, pivots, colours],
        smem=1,
        hbm=(1, 2, 3),
        scratch=rows[:2] + [pltpu.SemaphoreType.DMA((3, PARTS))],
        name="first",
        cost=pl.CostEstimate(flops=10**10, transcendentals=0, bytes_accessed=10**8),
    )
    kh, rt, alive, low = call(prep_body, prep_outs, [meta] + prep_ins, smem=1, name="prep")
    base = rhs
    for colour in (1, 2, 3):
        halo = halos(edge)
        load = False
        got = call(
            lambda *r, c=colour, l=load: turn_body(c, True, False, l, *r),
            ([(couplings.shape, F32)] + prep_outs if load else []) + [plain, field] + edges,
            [meta, couplings, pivots, colours, base, v, *halo] + (prep_ins if load else []),
            smem=1,
            hbm=(1,) if load else (),
            scratch=rows + ([pltpu.SemaphoreType.DMA((1, PARTS))] if load else []),
            name=f"forward{colour}",
            limit=16 << 20,
        )
        if load:
            couplings, kh, rt, alive, low, *got = got
        base, v, *edge = got
    for colour in (2, 1, 0):
        halo = halos(edge)
        final = colour == 0
        v, *edge = call(
            lambda *r, c=colour, f=final: turn_body(c, False, f, False, *r),
            [plain] if final else [field] + edges,
            [meta, couplings, pivots, colours, base, v, *halo],
            smem=1,
            scratch=rows,
            name=f"backward{colour}",
        )
    pairs = swaps(lax.axis_size("gy"), 0)
    cores = [[d for d in range(devices) if d % 2 == core] for core in range(2)]
    mine, other = call(
        terms_body, [((512, 128), F32)] * 2, [v, rt, kh, low, cells, perf_gather], name="terms", limit=24 << 20
    )
    mine = mine + lax.ppermute(other, "gy", pairs)
    got = lax.all_to_all(mine.reshape(64, 8, 128), axes, 0, 0, axis_index_groups=cores, tiled=True)
    (values,) = call(
        solve_body, [((64, 8, 128), F32)], [got, well_inverses.transpose(1, 2, 0), alive], name="solve"
    )
    mine = lax.all_to_all(values, axes, 0, 0, axis_index_groups=cores, tiled=True).reshape(512, 128)
    other = lax.ppermute(mine, "gy", pairs)
    return pl.pallas_call(
        return_body,
        out_shape=jax.ShapeDtypeStruct(plain[0], F32),
        in_specs=[VMEM_SPEC] * 8,
        out_specs=VMEM_SPEC,
        compiler_params=pltpu.CompilerParams(vmem_limit_bytes=24 << 20),
        name="back",
    )(*[in_vmem(x) for x in (mine, other, v, rt, kh, low, cells, perf_return)])


def solution(mesh):
    return jax.shard_map(
        shards,
        mesh=mesh,
        in_specs=(
            P(None, None, "gy", "gx"),
            P(None, None, None, None, "gy", "gx"),
            P(None, None, None, "gy", "gx"),
            P(None, "gy", "gx"),
            P(("gx", "gy")),
            P(("gx", "gy")),
            P(("gx", "gy")),
            P(None, ("gx", "gy")),
            P(None, ("gx", "gy")),
            P(),
            P(),
            P(("gx", "gy"), None, None),
        ),
        out_specs=P(None, None, "gy", "gx"),
        check_vma=False,
    )
```

```python
import jax
import jax.numpy as jnp
from jax import lax
from jax.experimental import pallas as pl
from jax.experimental.pallas import tpu as pltpu
from jax.sharding import PartitionSpec as P

F32 = jnp.float32
BF16 = jnp.bfloat16
UNROLL = 8
PARTS = 4
VMEM_SPEC = pl.BlockSpec(memory_space=pltpu.VMEM)
SMEM_SPEC = pl.BlockSpec(memory_space=pltpu.SMEM)


def iota(shape, dim):
    return lax.broadcasted_iota(jnp.int32, shape, dim)


def split(x):
    a = x.astype(BF16)
    return a, (x - a.astype(F32)).astype(BF16)


def dot(a, b, dims):
    return lax.dot_general(a, b, (dims, ((), ())), preferred_element_type=F32)


def in_vmem(x):
    return pltpu.with_memory_space_constraint(x, pltpu.VMEM)


def call(body, outs, ins, smem=0, hbm=(), scratch=(), name=None, limit=None, cost=None, alias=None):
    specs, args = [], []
    for k, x in enumerate(ins):
        if k < smem:
            specs.append(SMEM_SPEC)
        elif k in hbm:
            specs.append(pl.BlockSpec(memory_space=pltpu.HBM))
            x = pltpu.with_memory_space_constraint(x, pltpu.HBM)
        else:
            specs.append(VMEM_SPEC)
            x = in_vmem(x)
        args.append(x)
    return pl.pallas_call(
        body,
        out_shape=tuple(pltpu.VMEM(s, d) for s, d in outs),
        in_specs=specs,
        out_specs=tuple(VMEM_SPEC for _ in outs),
        scratch_shapes=list(scratch),
        compiler_params=pltpu.CompilerParams(vmem_limit_bytes=limit or (8 << 20)),
        cost_estimate=cost,
        input_output_aliases=alias or {},
        name=name,
    )(*args)


def emit_edges(new, z, nz, edges, ylo_ref, yhi_ref):
    xlo, xhi = edges
    lane = iota((8, 128), 1)
    for j in range(3):
        at = j * nz + z
        xlo = jnp.where(lane == at, pltpu.roll(new[j][:, :128], at, 1), xlo)
        xhi = jnp.where(lane == at, pltpu.roll(new[j][:, -128:], (at + 1) % 128, 1), xhi)
        ylo_ref[pl.ds(at, 1), :] = new[j][0:1, :]
        yhi_ref[pl.ds(at, 1), :] = new[j][-1:, :]
    return xlo, xhi


def store_edges(meta_ref, columns, ylo_ref, yhi_ref, xa_ref, xb_ref, ya_ref, yb_ref):
    x_odd = meta_ref[5] > 0
    y_odd = meta_ref[6] > 0
    xlo, xhi = columns
    xa_ref[...] = jnp.where(x_odd, xlo, xhi)
    xb_ref[...] = jnp.where(x_odd, xhi, xlo)
    ylo, yhi = ylo_ref[...], yhi_ref[...]
    ya_ref[...] = jnp.where(y_odd, ylo, yhi)
    yb_ref[...] = jnp.where(y_odd, yhi, ylo)


def zero_ends(ref, nz):
    zero = jnp.zeros(ref.shape[2:], F32)
    for j in range(3):
        ref[j, 0] = zero
        ref[j, nz + 1] = zero


def chunk_copies(pairs, sems, part, size, axes):
    out = []
    for k, ((src, dst), axis) in enumerate(zip(pairs, axes)):
        at = (slice(None),) * axis + (pl.ds(part * size, size),)
        out.append(pltpu.make_async_copy(src.at[at], dst.at[at], sems.at[k, part]))
    return out


def first_body(meta_ref, rhs_hbm, piv_hbm, col_hbm, rhs_ref, piv_ref, col_ref, v_ref, xa_ref, xb_ref, ya_ref, yb_ref, ylo_ref, yhi_ref, sems):
    nz = rhs_ref.shape[1]
    size = nz // PARTS
    pairs = [(rhs_hbm, rhs_ref), (piv_hbm, piv_ref), (col_hbm, col_ref)]
    for part in range(PARTS):
        for c in chunk_copies(pairs, sems, part, size, (1, 2, 0)):
            c.start()
    zero_ends(v_ref, nz)

    def step(z, edges):
        rhs = [rhs_ref[j, z] for j in range(3)]
        chosen = col_ref[z] == 0
        new = []
        for i in range(3):
            p = piv_ref[i, 0, z] * rhs[0] + piv_ref[i, 1, z] * rhs[1] + piv_ref[i, 2, z] * rhs[2]
            p = jnp.where(chosen, p, 0.0)
            v_ref[i, z + 1] = p
            new.append(p)
        return emit_edges(new, z, nz, edges, ylo_ref, yhi_ref)

    def block(part, edges):
        for c in chunk_copies(pairs, sems, part, size, (1, 2, 0)):
            c.wait()
        return lax.fori_loop(0, size, lambda k, e: step(part * size + k, e), edges, unroll=UNROLL)

    zero = jnp.zeros((8, 128), F32)
    edges = lax.fori_loop(0, PARTS, block, (zero, zero))
    store_edges(meta_ref, edges, ylo_ref, yhi_ref, xa_ref, xb_ref, ya_ref, yb_ref)


def turn_body(colour, forward, final, load, *refs):
    (meta_ref, coup_ref, piv_ref, col_ref, base_ref, v_ref, hxa_ref, hxb_ref, hya_ref, hyb_ref) = refs[:10]
    refs = list(refs[10:])
    if load:
        sems = refs.pop()
        prep_in, refs = refs[:5], refs[5:]
        coup_hbm, coup_ref = coup_ref, refs.pop(0)
        prep_out, refs = refs[:4], refs[4:]
    refs, (hylo_ref, hyhi_ref, ylo_ref, yhi_ref) = refs[:-4], refs[-4:]
    u_ref = refs.pop(0) if forward else None
    nv_ref, *edge_refs = refs
    nz = base_ref.shape[1]
    ny, nx = base_ref.shape[2:]
    size = nz // PARTS
    pairs = [(coup_hbm, coup_ref)] if load else []
    if load:
        for part in range(PARTS):
            for c in chunk_copies(pairs, sems, part, size, (3,)):
                c.start()
        prep_body(meta_ref, *prep_in, *prep_out)
    lane = iota((ny, 128), 1)
    row = iota((ny, nx), 0)
    first_lane, last_lane = lane == 0, lane == 127
    first_row, last_row = row == 0, row == ny - 1
    x_odd = meta_ref[5] > 0
    y_odd = meta_ref[6] > 0
    has = [meta_ref[k] > 0 for k in range(1, 5)]
    hxa, hxb = hxa_ref[...], hxb_ref[...]
    hxlo = jnp.where(has[0], jnp.where(x_odd, hxa, hxb), 0.0)
    hxhi = jnp.where(has[1], jnp.where(x_odd, hxb, hxa), 0.0)
    hya, hyb = hya_ref[...], hyb_ref[...]
    hylo_ref[...] = jnp.where(has[2], jnp.where(y_odd, hya, hyb), 0.0)
    hyhi_ref[...] = jnp.where(has[3], jnp.where(y_odd, hyb, hya), 0.0)
    if not final:
        zero_ends(nv_ref, nz)

    def step(z, edges):
        cur = [base_ref[j, z] for j in range(3)]
        base = list(cur)
        old = []
        for j in range(3):
            at = j * nz + z
            vc = v_ref[j, z + 1]
            old.append(vc)
            below = [pltpu.roll(vc[:, k : k + 128], 1, 1) for k in range(0, nx, 128)]
            above = [pltpu.roll(vc[:, k : k + 128], 127, 1) for k in range(0, nx, 128)]
            lead = [pltpu.roll(hxlo, (128 - at) % 128, 1)] + below[:-1]
            trail = above[1:] + [pltpu.roll(hxhi, 127 - at, 1)]
            xm = jnp.concatenate([jnp.where(first_lane, p, q) for p, q in zip(lead, below)], axis=1)
            xp = jnp.concatenate([jnp.where(last_lane, p, q) for p, q in zip(trail, above)], axis=1)
            ym = jnp.where(first_row, hylo_ref[pl.ds(at, 1), :], pltpu.roll(vc, 1, 0))
            yp = jnp.where(last_row, hyhi_ref[pl.ds(at, 1), :], pltpu.roll(vc, ny - 1, 0))
            zm = v_ref[j, z]
            zp = v_ref[j, z + 2]
            for i in range(3):
                t = coup_ref[0, i, j, z] * xm + coup_ref[1, i, j, z] * xp
                t = t + (coup_ref[2, i, j, z] * ym + coup_ref[3, i, j, z] * yp)
                t = t + (coup_ref[4, i, j, z] * zm + coup_ref[5, i, j, z] * zp)
                cur[i] = cur[i] - t
        chosen = col_ref[z] == colour
        new = []
        for i in range(3):
            p = piv_ref[i, 0, z] * cur[0] + piv_ref[i, 1, z] * cur[1] + piv_ref[i, 2, z] * cur[2]
            if forward:
                u_ref[i, z] = jnp.where(chosen, cur[i], base[i])
                keep_old = 0.0 if colour == 3 else old[i]
            else:
                keep_old = old[i]
            p = jnp.where(chosen, p, keep_old)
            if final:
                nv_ref[i, z] = p
            else:
                nv_ref[i, z + 1] = p
            new.append(p)
        if final:
            return edges
        return emit_edges(new, z, nz, edges, ylo_ref, yhi_ref)

    def block(part, edges):
        for c in chunk_copies(pairs, sems, part, size, (3,)):
            c.wait()
        return lax.fori_loop(0, size, lambda k, e: step(part * size + k, e), edges, unroll=UNROLL)

    zero = jnp.zeros((ny, 128), F32)
    if load:
        edges = lax.fori_loop(0, PARTS, block, (zero, zero))
    else:
        edges = lax.fori_loop(0, nz, step, (zero, zero), unroll=UNROLL)
    if not final:
        store_edges(meta_ref, edges, ylo_ref, yhi_ref, *edge_refs)


def both_ways(pairs):
    return [(a, b) for a, b in pairs] + [(b, a) for a, b in pairs]


def partners(nx, ny):
    at = lambda x, y: x * ny + y
    x_even = [(at(x, y), at(x + 1, y)) for x in range(0, nx, 2) for y in range(ny)]
    y_even = [(at(x, y), at(x, y + 1)) for y in range(0, ny, 2) for x in range(nx)]
    x_odd = [(at(x, y), at(x + 1, y)) for x in range(1, nx - 1, 2) for y in range(ny)]
    x_odd += [(at(x, y), at(x, y + 1)) for x in (0, nx - 1) for y in range(0, ny, 2)]
    y_odd = [(at(x, y), at(x, y + 1)) for y in range(1, ny - 1, 2) for x in range(nx)]
    y_odd += [(at(x, y), at(x + 1, y)) for y in (0, ny - 1) for x in range(0, nx, 2)]
    return [both_ways(p) for p in (x_even, x_odd, y_even, y_odd)]


def halos(edges):
    xa, xb, ya, yb = edges
    axes = ("gx", "gy")
    x_even, x_odd, y_even, y_odd = partners(lax.axis_size("gx"), lax.axis_size("gy"))
    hxb = lax.ppermute(xb, axes, x_odd)
    hyb = lax.ppermute(yb, axes, y_odd)
    hxa = lax.ppermute(xa, axes, x_even)
    hya = lax.ppermute(ya, axes, y_even)
    return hxa, hxb, hya, hyb


def one_hot_rows(ref, rows):
    n = ref.shape[1]
    step = jnp.broadcast_to(rows, (16, n)) - iota((16, n), 0)
    step = step.astype(jnp.int16)
    one, zero = jnp.ones((16, n), BF16), jnp.zeros((16, n), BF16)
    for at in range(0, ref.shape[0], 16):
        ref[at : at + 16, :] = jnp.where(step == jnp.int16(at), one, zero)


def prep_body(meta_ref, slot_ref, count_ref, cells_ref, wells_ref, segs_ref, kh_ref, rt_ref, alive_ref, lo_ref):
    n = cells_ref.shape[1]
    wells = wells_ref[...]
    table = slot_ref[...]
    pick = (iota((table.shape[0], n), 0) == (wells >> 7)).astype(BF16)
    high = dot((table >> 7).astype(F32).astype(BF16), pick, ((0,), (0,)))
    low = dot((table & 127).astype(F32).astype(BF16), pick, ((0,), (0,)))
    slot = jnp.where(iota((128, n), 0) == (wells & 127), high * 128.0 + low, 0.0)
    slot = jnp.sum(slot, axis=0, keepdims=True).astype(jnp.int32)
    segs = segs_ref[...]
    owner = slot >> 6
    tile = meta_ref[0]
    rows = ((owner ^ tile) & 1) * 512 + (owner >> 1) * 8 + (segs & 7)
    lo_ref[...] = (segs >> 3) * 64 + (slot & 63)
    one_hot_rows(kh_ref, rows)
    one_hot_rows(rt_ref, cells_ref[...] >> 8)
    own_slot = slot_ref[pl.ds(tile // 2, 1), :] - tile * 64
    own_count = jnp.broadcast_to(count_ref[pl.ds(tile // 2, 1), :].astype(F32), (8, 128)).astype(BF16)
    match = (iota((128, 128), 0) == own_slot).astype(F32).astype(BF16)
    counts = dot(own_count, match, ((1,), (1,)))
    alive_ref[0:8] = (iota((8, 128), 0).astype(F32) < counts).astype(F32)
    alive_ref[8:16] = ((iota((8, 128), 0) + 8).astype(F32) < counts).astype(F32)


def terms_body(s_ref, rt_ref, kh_ref, lo_ref, cells_ref, gather_ref, mine_ref, other_ref):
    n = cells_ref.shape[1]
    rt = rt_ref[...]
    at_col = iota((256, n), 0) == (cells_ref[...] & 255)
    term = jnp.zeros((1, n), F32)
    for i in range(3):
        f = s_ref[i].reshape(256, 256)
        g = sum(dot(h, rt, ((0,), (0,))) for h in split(f))
        v = jnp.sum(jnp.where(at_col, g, 0.0), axis=0, keepdims=True)
        term = term + gather_ref[pl.ds(i, 1), :] * v
    at_low = iota((128, n), 0) == lo_ref[...]
    stack = jnp.concatenate([jnp.where(at_low, h.astype(F32), 0.0).astype(BF16) for h in split(term)], axis=0)
    sums = dot(kh_ref[...], stack, ((1,), (1,)))
    sums = sums[:, :128] + sums[:, 128:]
    mine_ref[...] = sums[:512]
    other_ref[...] = sums[512:]


def solve_body(got_ref, inv_ref, alive_ref, out_ref):
    alive = alive_ref[:, :64]
    totals = jnp.sum(got_ref[...], axis=0)
    totals = jnp.concatenate([totals[:, :64], totals[:, 64:]], axis=0) * alive
    rows = [jnp.sum(inv_ref[i] * totals, axis=0, keepdims=True) for i in range(16)]
    values = jnp.concatenate(rows, axis=0) * alive
    values = jnp.concatenate([values[:8], values[8:]], axis=1)
    out_ref[...] = jnp.broadcast_to(values[None], out_ref.shape)


def return_body(mine_ref, other_ref, s_ref, rt_ref, kh_ref, lo_ref, cells_ref, back_ref, out_ref):
    n = cells_ref.shape[1]
    g = sum(dot(h, kh_ref[0:512], ((0,), (0,))) for h in split(mine_ref[...]))
    g = g + sum(dot(h, kh_ref[512:1024], ((0,), (0,))) for h in split(other_ref[...]))
    values = jnp.sum(jnp.where(iota((128, n), 0) == lo_ref[...], g, 0.0), axis=0, keepdims=True)
    at_col = iota((256, n), 0) == (cells_ref[...] & 255)
    rt = rt_ref[...]
    for i in range(3):
        w = back_ref[pl.ds(i, 1), :] * values
        change = sum(
            dot(rt, jnp.where(at_col, h.astype(F32), 0.0).astype(BF16), ((1,), (1,))) for h in split(w)
        )
        out_ref[i] = s_ref[i] - change.reshape(32, 8, 256)


def shards(
    rhs,
    couplings,
    pivots,
    colours,
    perf_cells,
    perf_wells,
    perf_segments,
    perf_gather,
    perf_return,
    well_slot,
    seg_count,
    well_inverses,
):
    axes = ("gx", "gy")
    devices = lax.axis_size(axes)
    gx = lax.axis_index("gx")
    gy = lax.axis_index("gy")
    tile = lax.axis_index(axes)
    meta = jnp.stack(
        [
            tile,
            gx > 0,
            gx < lax.axis_size("gx") - 1,
            gy > 0,
            gy < lax.axis_size("gy") - 1,
            gx % 2,
            gy % 2,
        ]
    ).astype(jnp.int32)
    _, nz, ny, nx = rhs.shape
    field = ((3, nz + 2, ny, nx), F32)
    plain = ((3, nz, ny, nx), F32)
    edges = [((ny, 128), F32)] * 2 + [((3 * nz, nx), F32)] * 2
    n = perf_cells.shape[0]
    cells = perf_cells.reshape(1, n)
    rows = [pltpu.VMEM((3 * nz, nx), F32)] * 4
    prep_ins = [
        well_slot.reshape(-1, 128),
        seg_count.reshape(-1, 128),
        cells,
        perf_wells.reshape(1, n),
        perf_segments.reshape(1, n),
    ]
    prep_outs = [((1024, n), BF16), ((256, n), BF16), ((16, 128), F32), ((1, n), jnp.int32)]

    rhs, pivots, colours, v, *edge = call(
        first_body,
        [plain, (pivots.shape, F32), (colours.shape, jnp.int32), field] + edges,
        [meta, rhs, pivots, colours],
        smem=1,
        hbm=(1, 2, 3),
        scratch=rows[:2] + [pltpu.SemaphoreType.DMA((3, PARTS))],
        name="first",
        cost=pl.CostEstimate(flops=10**10, transcendentals=0, bytes_accessed=10**8),
    )
    kh, rt, alive, low = call(prep_body, prep_outs, [meta] + prep_ins, smem=1, name="prep")
    base = rhs
    for colour in (1, 2, 3):
        halo = halos(edge)
        load = False
        got = call(
            lambda *r, c=colour, l=load: turn_body(c, True, False, l, *r),
            ([(couplings.shape, F32)] + prep_outs if load else []) + [plain, field] + edges,
            [meta, couplings, pivots, colours, base, v, *halo] + (prep_ins if load else []),
            smem=1,
            hbm=(1,) if load else (),
            scratch=rows + ([pltpu.SemaphoreType.DMA((1, PARTS))] if load else []),
            name=f"forward{colour}",
            limit=16 << 20,
        )
        if load:
            couplings, kh, rt, alive, low, *got = got
        base, v, *edge = got
    for colour in (2, 1, 0):
        halo = halos(edge)
        final = colour == 0
        v, *edge = call(
            lambda *r, c=colour, f=final: turn_body(c, False, f, False, *r),
            [plain] if final else [field] + edges,
            [meta, couplings, pivots, colours, base, v, *halo],
            smem=1,
            scratch=rows,
            name=f"backward{colour}",
        )
    pairs = partners(lax.axis_size("gx"), lax.axis_size("gy"))[2]
    cores = [[d for d in range(devices) if d % 2 == core] for core in range(2)]
    mine, other = call(
        terms_body, [((512, 128), F32)] * 2, [v, rt, kh, low, cells, perf_gather], name="terms", limit=24 << 20
    )
    mine = mine + lax.ppermute(other, axes, pairs)
    got = lax.all_to_all(mine.reshape(64, 8, 128), axes, 0, 0, axis_index_groups=cores, tiled=True)
    (values,) = call(
        solve_body, [((64, 8, 128), F32)], [got, well_inverses.transpose(1, 2, 0), alive], name="solve"
    )
    mine = lax.all_to_all(values, axes, 0, 0, axis_index_groups=cores, tiled=True).reshape(512, 128)
    other = lax.ppermute(mine, axes, pairs)
    return pl.pallas_call(
        return_body,
        out_shape=jax.ShapeDtypeStruct(plain[0], F32),
        in_specs=[VMEM_SPEC] * 8,
        out_specs=VMEM_SPEC,
        compiler_params=pltpu.CompilerParams(vmem_limit_bytes=24 << 20),
        name="back",
    )(*[in_vmem(x) for x in (mine, other, v, rt, kh, low, cells, perf_return)])


def solution(mesh):
    return jax.shard_map(
        shards,
        mesh=mesh,
        in_specs=(
            P(None, None, "gy", "gx"),
            P(None, None, None, None, "gy", "gx"),
            P(None, None, None, "gy", "gx"),
            P(None, "gy", "gx"),
            P(("gx", "gy")),
            P(("gx", "gy")),
            P(("gx", "gy")),
            P(None, ("gx", "gy")),
            P(None, ("gx", "gy")),
            P(),
            P(),
            P(("gx", "gy"), None, None),
        ),
        out_specs=P(None, None, "gy", "gx"),
        check_vma=False,
    )
```

```python
import jax
import jax.numpy as jnp
from jax import lax
from jax.experimental import pallas as pl
from jax.experimental.pallas import tpu as pltpu
from jax.sharding import PartitionSpec as P

F32 = jnp.float32
BF16 = jnp.bfloat16
UNROLL = 8
PARTS = 4
VMEM_SPEC = pl.BlockSpec(memory_space=pltpu.VMEM)
SMEM_SPEC = pl.BlockSpec(memory_space=pltpu.SMEM)


def iota(shape, dim):
    return lax.broadcasted_iota(jnp.int32, shape, dim)


def split(x):
    a = x.astype(BF16)
    return a, (x - a.astype(F32)).astype(BF16)


def dot(a, b, dims):
    return lax.dot_general(a, b, (dims, ((), ())), preferred_element_type=F32)


def in_vmem(x):
    return pltpu.with_memory_space_constraint(x, pltpu.VMEM)


def call(body, outs, ins, smem=0, hbm=(), scratch=(), name=None, limit=None, cost=None, alias=None):
    specs, args = [], []
    for k, x in enumerate(ins):
        if k < smem:
            specs.append(SMEM_SPEC)
        elif k in hbm:
            specs.append(pl.BlockSpec(memory_space=pltpu.HBM))
            x = pltpu.with_memory_space_constraint(x, pltpu.HBM)
        else:
            specs.append(VMEM_SPEC)
            x = in_vmem(x)
        args.append(x)
    return pl.pallas_call(
        body,
        out_shape=tuple(pltpu.VMEM(s, d) for s, d in outs),
        in_specs=specs,
        out_specs=tuple(VMEM_SPEC for _ in outs),
        scratch_shapes=list(scratch),
        compiler_params=pltpu.CompilerParams(vmem_limit_bytes=limit or (8 << 20)),
        cost_estimate=cost,
        input_output_aliases=alias or {},
        name=name,
    )(*args)


def emit_edges(meta_ref, v_ref, xa_ref, xb_ref, ya_ref, yb_ref):
    _, layers, ny, nx = v_ref.shape
    nz = layers - 2
    x_odd = meta_ref[5] > 0
    y_odd = meta_ref[6] > 0
    lane = iota((ny, 128), 1)
    low_x = [jnp.zeros((ny, 128), F32)] * 4
    high_x = [jnp.zeros((ny, 128), F32)] * 4
    for j in range(3):
        low = jnp.concatenate([v_ref[j, z + 1, 0:1, :] for z in range(nz)], axis=0)
        high = jnp.concatenate([v_ref[j, z + 1, ny - 1 : ny, :] for z in range(nz)], axis=0)
        ya_ref[j * nz : (j + 1) * nz, :] = jnp.where(y_odd, low, high)
        yb_ref[j * nz : (j + 1) * nz, :] = jnp.where(y_odd, high, low)
        for z in range(nz):
            to = j * nz + z
            here = lane == to
            k = z % 4
            low_x[k] = jnp.where(here, pltpu.roll(v_ref[j, z + 1, :, :128], to, 1), low_x[k])
            high_x[k] = jnp.where(here, pltpu.roll(v_ref[j, z + 1, :, nx - 128 :], (to + 1) % 128, 1), high_x[k])
    xlo, xhi = sum(low_x), sum(high_x)
    xa_ref[...] = jnp.where(x_odd, xlo, xhi)
    xb_ref[...] = jnp.where(x_odd, xhi, xlo)


def zero_ends(ref, nz):
    zero = jnp.zeros(ref.shape[2:], F32)
    for j in range(3):
        ref[j, 0] = zero
        ref[j, nz + 1] = zero


def chunk_copies(pairs, sems, part, size, axes):
    out = []
    for k, ((src, dst), axis) in enumerate(zip(pairs, axes)):
        at = (slice(None),) * axis + (pl.ds(part * size, size),)
        out.append(pltpu.make_async_copy(src.at[at], dst.at[at], sems.at[k, part]))
    return out


def first_body(meta_ref, rhs_hbm, piv_hbm, col_hbm, rhs_ref, piv_ref, col_ref, v_ref, xa_ref, xb_ref, ya_ref, yb_ref, sems):
    nz = rhs_ref.shape[1]
    size = nz // PARTS
    pairs = [(rhs_hbm, rhs_ref), (piv_hbm, piv_ref), (col_hbm, col_ref)]
    for part in range(PARTS):
        for c in chunk_copies(pairs, sems, part, size, (1, 2, 0)):
            c.start()
    zero_ends(v_ref, nz)

    def step(z, carry):
        rhs = [rhs_ref[j, z] for j in range(3)]
        chosen = col_ref[z] == 0
        for i in range(3):
            p = piv_ref[i, 0, z] * rhs[0] + piv_ref[i, 1, z] * rhs[1] + piv_ref[i, 2, z] * rhs[2]
            p = jnp.where(chosen, p, 0.0)
            v_ref[i, z + 1] = p
        return carry

    def block(part, carry):
        for c in chunk_copies(pairs, sems, part, size, (1, 2, 0)):
            c.wait()
        return lax.fori_loop(0, size, lambda k, e: step(part * size + k, e), carry, unroll=UNROLL)

    lax.fori_loop(0, PARTS, block, 0)
    emit_edges(meta_ref, v_ref, xa_ref, xb_ref, ya_ref, yb_ref)


def turn_body(colour, forward, final, load, *refs):
    (meta_ref, coup_ref, piv_ref, col_ref, base_ref, v_ref, hxa_ref, hxb_ref, hya_ref, hyb_ref) = refs[:10]
    refs = list(refs[10:])
    if load:
        sems = refs.pop()
        prep_in, refs = refs[:5], refs[5:]
        coup_hbm, coup_ref = coup_ref, refs.pop(0)
        prep_out, refs = refs[:4], refs[4:]
    refs, (hylo_ref, hyhi_ref) = refs[:-2], refs[-2:]
    u_ref = refs.pop(0) if forward else None
    nv_ref, *edge_refs = refs
    nz = base_ref.shape[1]
    ny, nx = base_ref.shape[2:]
    size = nz // PARTS
    pairs = [(coup_hbm, coup_ref)] if load else []
    if load:
        for part in range(PARTS):
            for c in chunk_copies(pairs, sems, part, size, (3,)):
                c.start()
        prep_body(meta_ref, *prep_in, *prep_out)
    lane = iota((ny, 128), 1)
    row = iota((ny, nx), 0)
    first_lane, last_lane = lane == 0, lane == 127
    first_row, last_row = row == 0, row == ny - 1
    x_odd = meta_ref[5] > 0
    y_odd = meta_ref[6] > 0
    has = [meta_ref[k] > 0 for k in range(1, 5)]
    hxa, hxb = hxa_ref[...], hxb_ref[...]
    hxlo = jnp.where(has[0], jnp.where(x_odd, hxa, hxb), 0.0)
    hxhi = jnp.where(has[1], jnp.where(x_odd, hxb, hxa), 0.0)
    hya, hyb = hya_ref[...], hyb_ref[...]
    hylo_ref[...] = jnp.where(has[2], jnp.where(y_odd, hya, hyb), 0.0)
    hyhi_ref[...] = jnp.where(has[3], jnp.where(y_odd, hyb, hya), 0.0)
    if not final:
        zero_ends(nv_ref, nz)

    def step(z, carry):
        cur = [base_ref[j, z] for j in range(3)]
        base = list(cur)
        old = []
        for j in range(3):
            at = j * nz + z
            vc = v_ref[j, z + 1]
            old.append(vc)
            below = [pltpu.roll(vc[:, k : k + 128], 1, 1) for k in range(0, nx, 128)]
            above = [pltpu.roll(vc[:, k : k + 128], 127, 1) for k in range(0, nx, 128)]
            lead = [pltpu.roll(hxlo, (128 - at) % 128, 1)] + below[:-1]
            trail = above[1:] + [pltpu.roll(hxhi, 127 - at, 1)]
            xm = jnp.concatenate([jnp.where(first_lane, p, q) for p, q in zip(lead, below)], axis=1)
            xp = jnp.concatenate([jnp.where(last_lane, p, q) for p, q in zip(trail, above)], axis=1)
            ym = jnp.where(first_row, hylo_ref[pl.ds(at, 1), :], pltpu.roll(vc, 1, 0))
            yp = jnp.where(last_row, hyhi_ref[pl.ds(at, 1), :], pltpu.roll(vc, ny - 1, 0))
            zm = v_ref[j, z]
            zp = v_ref[j, z + 2]
            for i in range(3):
                t = coup_ref[0, i, j, z] * xm + coup_ref[1, i, j, z] * xp
                t = t + (coup_ref[2, i, j, z] * ym + coup_ref[3, i, j, z] * yp)
                t = t + (coup_ref[4, i, j, z] * zm + coup_ref[5, i, j, z] * zp)
                cur[i] = cur[i] - t
        chosen = col_ref[z] == colour
        for i in range(3):
            p = piv_ref[i, 0, z] * cur[0] + piv_ref[i, 1, z] * cur[1] + piv_ref[i, 2, z] * cur[2]
            if forward:
                u_ref[i, z] = jnp.where(chosen, cur[i], base[i])
                keep_old = 0.0 if colour == 3 else old[i]
            else:
                keep_old = old[i]
            p = jnp.where(chosen, p, keep_old)
            if final:
                nv_ref[i, z] = p
            else:
                nv_ref[i, z + 1] = p
        return carry

    def block(part, carry):
        for c in chunk_copies(pairs, sems, part, size, (3,)):
            c.wait()
        return lax.fori_loop(0, size, lambda k, e: step(part * size + k, e), carry, unroll=UNROLL)

    if load:
        lax.fori_loop(0, PARTS, block, 0)
    else:
        lax.fori_loop(0, nz, step, 0, unroll=UNROLL)
    if not final:
        emit_edges(meta_ref, nv_ref, *edge_refs)


def both_ways(pairs):
    return [(a, b) for a, b in pairs] + [(b, a) for a, b in pairs]


def partners(nx, ny):
    at = lambda x, y: x * ny + y
    x_even = [(at(x, y), at(x + 1, y)) for x in range(0, nx, 2) for y in range(ny)]
    y_even = [(at(x, y), at(x, y + 1)) for y in range(0, ny, 2) for x in range(nx)]
    x_odd = [(at(x, y), at(x + 1, y)) for x in range(1, nx - 1, 2) for y in range(ny)]
    x_odd += [(at(x, y), at(x, y + 1)) for x in (0, nx - 1) for y in range(0, ny, 2)]
    y_odd = [(at(x, y), at(x, y + 1)) for y in range(1, ny - 1, 2) for x in range(nx)]
    y_odd += [(at(x, y), at(x + 1, y)) for y in (0, ny - 1) for x in range(0, nx, 2)]
    return [both_ways(p) for p in (x_even, x_odd, y_even, y_odd)]


def halos(edges):
    xa, xb, ya, yb = edges
    axes = ("gx", "gy")
    x_even, x_odd, y_even, y_odd = partners(lax.axis_size("gx"), lax.axis_size("gy"))
    hxb = lax.ppermute(xb, axes, x_odd)
    hyb = lax.ppermute(yb, axes, y_odd)
    hxa = lax.ppermute(xa, axes, x_even)
    hya = lax.ppermute(ya, axes, y_even)
    return hxa, hxb, hya, hyb


def one_hot_rows(ref, rows):
    n = ref.shape[1]
    step = jnp.broadcast_to(rows, (16, n)) - iota((16, n), 0)
    step = step.astype(jnp.int16)
    one, zero = jnp.ones((16, n), BF16), jnp.zeros((16, n), BF16)
    for at in range(0, ref.shape[0], 16):
        ref[at : at + 16, :] = jnp.where(step == jnp.int16(at), one, zero)


def prep_body(meta_ref, slot_ref, count_ref, cells_ref, wells_ref, segs_ref, kh_ref, rt_ref, alive_ref, lo_ref):
    n = cells_ref.shape[1]
    wells = wells_ref[...]
    table = slot_ref[...]
    pick = (iota((table.shape[0], n), 0) == (wells >> 7)).astype(BF16)
    high = dot((table >> 7).astype(F32).astype(BF16), pick, ((0,), (0,)))
    low = dot((table & 127).astype(F32).astype(BF16), pick, ((0,), (0,)))
    slot = jnp.where(iota((128, n), 0) == (wells & 127), high * 128.0 + low, 0.0)
    slot = jnp.sum(slot, axis=0, keepdims=True).astype(jnp.int32)
    segs = segs_ref[...]
    owner = slot >> 6
    tile = meta_ref[0]
    rows = ((owner ^ tile) & 1) * 512 + (owner >> 1) * 8 + (segs & 7)
    lo_ref[...] = (segs >> 3) * 64 + (slot & 63)
    one_hot_rows(kh_ref, rows)
    one_hot_rows(rt_ref, cells_ref[...] >> 8)
    own_slot = slot_ref[pl.ds(tile // 2, 1), :] - tile * 64
    own_count = jnp.broadcast_to(count_ref[pl.ds(tile // 2, 1), :].astype(F32), (8, 128)).astype(BF16)
    match = (iota((128, 128), 0) == own_slot).astype(F32).astype(BF16)
    counts = dot(own_count, match, ((1,), (1,)))
    alive_ref[0:8] = (iota((8, 128), 0).astype(F32) < counts).astype(F32)
    alive_ref[8:16] = ((iota((8, 128), 0) + 8).astype(F32) < counts).astype(F32)


def terms_body(s_ref, rt_ref, kh_ref, lo_ref, cells_ref, gather_ref, mine_ref, other_ref):
    n = cells_ref.shape[1]
    rt = rt_ref[...]
    at_col = iota((256, n), 0) == (cells_ref[...] & 255)
    term = jnp.zeros((1, n), F32)
    for i in range(3):
        f = s_ref[i].reshape(256, 256)
        g = sum(dot(h, rt, ((0,), (0,))) for h in split(f))
        v = jnp.sum(jnp.where(at_col, g, 0.0), axis=0, keepdims=True)
        term = term + gather_ref[pl.ds(i, 1), :] * v
    at_low = iota((128, n), 0) == lo_ref[...]
    stack = jnp.concatenate([jnp.where(at_low, h.astype(F32), 0.0).astype(BF16) for h in split(term)], axis=0)
    sums = dot(kh_ref[...], stack, ((1,), (1,)))
    sums = sums[:, :128] + sums[:, 128:]
    mine_ref[...] = sums[:512]
    other_ref[...] = sums[512:]


def solve_body(got_ref, inv_ref, alive_ref, out_ref):
    alive = alive_ref[:, :64]
    totals = jnp.sum(got_ref[...], axis=0)
    totals = jnp.concatenate([totals[:, :64], totals[:, 64:]], axis=0) * alive
    rows = [jnp.sum(inv_ref[i] * totals, axis=0, keepdims=True) for i in range(16)]
    values = jnp.concatenate(rows, axis=0) * alive
    values = jnp.concatenate([values[:8], values[8:]], axis=1)
    out_ref[...] = jnp.broadcast_to(values[None], out_ref.shape)


def return_body(mine_ref, other_ref, s_ref, rt_ref, kh_ref, lo_ref, cells_ref, back_ref, out_ref):
    n = cells_ref.shape[1]
    g = sum(dot(h, kh_ref[0:512], ((0,), (0,))) for h in split(mine_ref[...]))
    g = g + sum(dot(h, kh_ref[512:1024], ((0,), (0,))) for h in split(other_ref[...]))
    values = jnp.sum(jnp.where(iota((128, n), 0) == lo_ref[...], g, 0.0), axis=0, keepdims=True)
    at_col = iota((256, n), 0) == (cells_ref[...] & 255)
    rt = rt_ref[...]
    for i in range(3):
        w = back_ref[pl.ds(i, 1), :] * values
        change = sum(
            dot(rt, jnp.where(at_col, h.astype(F32), 0.0).astype(BF16), ((1,), (1,))) for h in split(w)
        )
        out_ref[i] = s_ref[i] - change.reshape(32, 8, 256)


def shards(
    rhs,
    couplings,
    pivots,
    colours,
    perf_cells,
    perf_wells,
    perf_segments,
    perf_gather,
    perf_return,
    well_slot,
    seg_count,
    well_inverses,
):
    axes = ("gx", "gy")
    devices = lax.axis_size(axes)
    gx = lax.axis_index("gx")
    gy = lax.axis_index("gy")
    tile = lax.axis_index(axes)
    meta = jnp.stack(
        [
            tile,
            gx > 0,
            gx < lax.axis_size("gx") - 1,
            gy > 0,
            gy < lax.axis_size("gy") - 1,
            gx % 2,
            gy % 2,
        ]
    ).astype(jnp.int32)
    _, nz, ny, nx = rhs.shape
    field = ((3, nz + 2, ny, nx), F32)
    plain = ((3, nz, ny, nx), F32)
    edges = [((ny, 128), F32)] * 2 + [((3 * nz, nx), F32)] * 2
    n = perf_cells.shape[0]
    cells = perf_cells.reshape(1, n)
    rows = [pltpu.VMEM((3 * nz, nx), F32)] * 2
    prep_ins = [
        well_slot.reshape(-1, 128),
        seg_count.reshape(-1, 128),
        cells,
        perf_wells.reshape(1, n),
        perf_segments.reshape(1, n),
    ]
    prep_outs = [((1024, n), BF16), ((256, n), BF16), ((16, 128), F32), ((1, n), jnp.int32)]

    rhs, pivots, colours, v, *edge = call(
        first_body,
        [plain, (pivots.shape, F32), (colours.shape, jnp.int32), field] + edges,
        [meta, rhs, pivots, colours],
        smem=1,
        hbm=(1, 2, 3),
        scratch=[pltpu.SemaphoreType.DMA((3, PARTS))],
        name="first",
        cost=pl.CostEstimate(flops=10**10, transcendentals=0, bytes_accessed=10**8),
    )
    kh, rt, alive, low = call(prep_body, prep_outs, [meta] + prep_ins, smem=1, name="prep")
    base = rhs
    for colour in (1, 2, 3):
        halo = halos(edge)
        load = False
        got = call(
            lambda *r, c=colour, l=load: turn_body(c, True, False, l, *r),
            ([(couplings.shape, F32)] + prep_outs if load else []) + [plain, field] + edges,
            [meta, couplings, pivots, colours, base, v, *halo] + (prep_ins if load else []),
            smem=1,
            hbm=(1,) if load else (),
            scratch=rows + ([pltpu.SemaphoreType.DMA((1, PARTS))] if load else []),
            name=f"forward{colour}",
            limit=16 << 20,
        )
        if load:
            couplings, kh, rt, alive, low, *got = got
        base, v, *edge = got
    for colour in (2, 1, 0):
        halo = halos(edge)
        final = colour == 0
        v, *edge = call(
            lambda *r, c=colour, f=final: turn_body(c, False, f, False, *r),
            [plain] if final else [field] + edges,
            [meta, couplings, pivots, colours, base, v, *halo],
            smem=1,
            scratch=rows,
            name=f"backward{colour}",
        )
    pairs = partners(lax.axis_size("gx"), lax.axis_size("gy"))[2]
    cores = [[d for d in range(devices) if d % 2 == core] for core in range(2)]
    mine, other = call(
        terms_body, [((512, 128), F32)] * 2, [v, rt, kh, low, cells, perf_gather], name="terms", limit=24 << 20
    )
    mine = mine + lax.ppermute(other, axes, pairs)
    got = lax.all_to_all(mine.reshape(64, 8, 128), axes, 0, 0, axis_index_groups=cores, tiled=True)
    (values,) = call(
        solve_body, [((64, 8, 128), F32)], [got, well_inverses.transpose(1, 2, 0), alive], name="solve"
    )
    mine = lax.all_to_all(values, axes, 0, 0, axis_index_groups=cores, tiled=True).reshape(512, 128)
    other = lax.ppermute(mine, axes, pairs)
    return pl.pallas_call(
        return_body,
        out_shape=jax.ShapeDtypeStruct(plain[0], F32),
        in_specs=[VMEM_SPEC] * 8,
        out_specs=VMEM_SPEC,
        compiler_params=pltpu.CompilerParams(vmem_limit_bytes=24 << 20),
        name="back",
    )(*[in_vmem(x) for x in (mine, other, v, rt, kh, low, cells, perf_return)])


def solution(mesh):
    return jax.shard_map(
        shards,
        mesh=mesh,
        in_specs=(
            P(None, None, "gy", "gx"),
            P(None, None, None, None, "gy", "gx"),
            P(None, None, None, "gy", "gx"),
            P(None, "gy", "gx"),
            P(("gx", "gy")),
            P(("gx", "gy")),
            P(("gx", "gy")),
            P(None, ("gx", "gy")),
            P(None, ("gx", "gy")),
            P(),
            P(),
            P(("gx", "gy"), None, None),
        ),
        out_specs=P(None, None, "gy", "gx"),
        check_vma=False,
    )
```
